128 devices in a mesh: sector: 16 (over z, x_lo, core), tm: 2 (over x_hi), space: 4 (over y).
Axes of the slice: x: 4 (x_hi: 2, x_lo: 2; x = x_hi * 2 + x_lo), y: 4, z: 4, core: 2. Of those that a mesh axis runs over, the one named last changes fastest.
Arguments:
- records: bfloat16 [16, 592, 3, 8192], P('sector', 'tm', None, 'space'), may hold values from -6 to 6
- block_start: int32 [16], replicated, may hold values from 0 to 231, as said below
- slab_index: int32 [8192], P('space'), may hold values from 0 to 15
- weight_table: float32 [16], replicated, may hold values from 0.25 to 4
Outputs:
- mode_fields: bfloat16 [8, 32, 2, 8, 3, 8192], P(None, ('sector', 'tm'), None, None, None, 'space')
- energy: float32 [8, 32, 8], P(None, ('sector', 'tm'))
The draws below stay inside these ranges and needn't reach their ends.
Inputs may be any that keep to these rules, and one draw needn't show every extreme that they name: `block_start`: block j of each record (j < 8) starts at j * 32 plus 0 to 7 snapshots.
All inputs are finite; a program needn't handle non-finite values.
Results may differ from the reference program's by a relative error of at most 0.02.
Values may be sent and summed in bfloat16 or wider, within the bound.
A program may use at most 64 MiB of HBM per device.

```python
import math
import jax
import jax.numpy as jnp
from jax import lax

NFFT = 64
NFREQ = 32
SECTORS = 16
ORDERS = 8
FIELDS = 3
MODES = 8
SUBIT = 4
NSLAB = 16
BLK_DEV = 8
TREC = 296
BLOCKS = 16
TIME = 592
CELLS = 8192


def draw_block_start(key, part):
    jitter = jax.random.randint(key, (BLOCKS,), 0, NFFT // 8, dtype=jnp.int32)
    jitter = jitter.at[0].set(0).at[BLOCKS - 1].set(NFFT // 8 - 1)
    base = jnp.arange(BLOCKS, dtype=jnp.int32) % BLK_DEV * (NFFT // 2)
    return (base + jitter).astype(jnp.int32)


def with_ends(entries, own_key, smallest, high):
    extent = entries.shape
    index_at = [jax.random.randint(jax.random.fold_in(own_key, axis), (), 0, extent[axis]) for axis in range(len(extent))]
    entries = entries.at[tuple(index_at)].set(smallest)
    longest = extent.index(max(extent))
    index_at[longest] = (index_at[longest] + 1) % extent[longest]
    return entries.at[tuple(index_at)].set(high)


def shard_levels(own_key, shape, pieces, low, top_value):
    gain, own = 1.0, jax.random.fold_in(own_key, 6)
    for position, shards_of in pieces:
        heights = jnp.exp(jax.random.uniform(jax.random.fold_in(own, position), (shards_of,), jnp.float32, low / len(pieces), top_value / len(pieces)))
        gain = gain * jnp.repeat(heights, shape[position] // shards_of).reshape([-1 if axis == position else 1 for axis in range(len(shape))])
    return gain


def noise(rng, extent, deviation, bound, shards=(), held_as=jnp.bfloat16):
    entries = jax.random.normal(rng, extent, jnp.float32) * deviation
    if len(shards) > 0:
        entries = shard_levels(rng, extent, shards, -0.22, 0.18) * entries
    return jnp.clip(entries, min=-bound, max=bound).astype(held_as)


def setup_inputs(seed: int = 0) -> dict:
    seeds = jax.random.split(jax.random.key(seed), 5)
    return {
        "records": noise(seeds[0], (SECTORS, TIME, FIELDS, CELLS), 1.0, 6.0, ((0, 16), (1, 2), (3, 4))),
        "block_start": draw_block_start(jax.random.fold_in(seeds[4], 71), 0),
        "slab_index": with_ends(jax.random.randint(seeds[2], (CELLS,), 0, NSLAB), jax.random.fold_in(seeds[2], 1), 0, NSLAB - 1).astype(jnp.int32),
        "weight_table": jnp.clip(jnp.exp(jax.random.uniform(seeds[3], (NSLAB,), jnp.float32, math.log(0.25), math.log(4.0))), 0.25, 4.0),
    }


EPSILON = 1e-06

def time_table(length, freq_count):
    steps_t = jnp.arange(length, dtype=jnp.float32)
    freq_f = jnp.arange(freq_count, dtype=jnp.float32)
    window = 0.5 - 0.5 * jnp.cos(2.0 * math.pi * steps_t / length)
    angles = 2.0 * math.pi * freq_f[:, None] * steps_t[None, :] / length
    both = jnp.stack([window * jnp.cos(angles), -window * jnp.sin(angles)])
    return (both / math.sqrt(length)).astype(jnp.bfloat16)

def order_table(orders, sectors):
    order_m = jnp.arange(orders, dtype=jnp.float32)[:, None]
    sector_s = jnp.arange(sectors, dtype=jnp.float32)[None, :]
    angles = 2.0 * math.pi * order_m * sector_s / sectors
    cosine = jnp.cos(angles)
    sine_part = jnp.sin(angles)
    upper_row = jnp.stack([cosine, sine_part], -1)
    lower_row = jnp.stack([-sine_part, cosine], -1)
    return (jnp.stack([upper_row, lower_row], 1) / math.sqrt(sectors)).astype(jnp.bfloat16)

def matmul_high(left_side, right_side):
    return jnp.matmul(left_side, right_side, precision=lax.Precision.HIGHEST)

def subspace(gram_re, gram_im):
    order_size = gram_re.shape[-1]
    basis_re = jnp.broadcast_to(jnp.eye(order_size, MODES, dtype=jnp.float32), gram_re.shape[:-1] + (MODES,))
    basis_im = jnp.zeros_like(basis_re)
    for sweep in range(SUBIT):
        image_re = matmul_high(gram_re, basis_re) - matmul_high(gram_im, basis_im)
        image_im = matmul_high(gram_re, basis_im) + matmul_high(gram_im, basis_re)
        done_re = []
        done_im = []
        for column in range(MODES):
            vec_re = image_re[..., column]
            vec_im = image_im[..., column]
            for earlier in range(column):
                old_re = done_re[earlier]
                old_im = done_im[earlier]
                proj_re = lax.optimization_barrier(jnp.sum(old_re * vec_re + old_im * vec_im, -1, keepdims=True))
                proj_im = lax.optimization_barrier(jnp.sum(old_re * vec_im - old_im * vec_re, -1, keepdims=True))
                vec_re = vec_re - (proj_re * old_re - proj_im * old_im)
                vec_im = vec_im - (proj_re * old_im + proj_im * old_re)
            length_v = jnp.sqrt(lax.optimization_barrier(jnp.sum(vec_re * vec_re + vec_im * vec_im, -1, keepdims=True)) + EPSILON)
            done_re.append(vec_re / length_v)
            done_im.append(vec_im / length_v)
        basis_re = jnp.stack(done_re, -1)
        basis_im = jnp.stack(done_im, -1)
    return (basis_re, basis_im)

def reference(records, block_start, slab_index, weight_table):
    time_basis = time_table(NFFT, NFREQ).astype(jnp.float32)
    azimuth = order_table(ORDERS, SECTORS).astype(jnp.float32)
    weight = weight_table[slab_index]
    cell_total = FIELDS * CELLS
    starts_abs = jnp.arange(BLOCKS, dtype=jnp.int32) // BLK_DEV * TREC + block_start.astype(jnp.int32)

    def one_freq(freq):
        freq_row = lax.dynamic_index_in_dim(time_basis, freq, 1, keepdims=False)

        def one_block(start_at):
            segment = lax.dynamic_slice_in_dim(records, start_at, NFFT, 1).astype(jnp.float32)
            return jnp.einsum('ct,stkx->sckx', freq_row, segment).astype(jnp.bfloat16)
        spectra = lax.map(one_block, starts_abs)
        spectra = lax.optimization_barrier(spectra).astype(jnp.float32)
        coeffs = jnp.einsum('mcse,bsekx->mcbkx', azimuth, spectra).astype(jnp.bfloat16)
        coeffs = lax.optimization_barrier(coeffs)
        coeffs_wide = coeffs.astype(jnp.float32)
        weighted = lax.optimization_barrier((coeffs_wide * weight).astype(jnp.bfloat16)).astype(jnp.float32)
        products = jnp.einsum('mcbkx,mdekx->mcbde', weighted, coeffs_wide)
        gram_re = products[:, 0, :, 0, :] + products[:, 1, :, 1, :]
        gram_im = products[:, 0, :, 1, :] - products[:, 1, :, 0, :]
        basis_re, basis_im = subspace(gram_re, gram_im)
        image_re = matmul_high(gram_re, basis_re) - matmul_high(gram_im, basis_im)
        image_im = matmul_high(gram_re, basis_im) + matmul_high(gram_im, basis_re)
        energy = lax.optimization_barrier(jnp.sum(basis_re * image_re + basis_im * image_im, -2)) / cell_total
        short_re = lax.optimization_barrier(basis_re.astype(jnp.bfloat16)).astype(jnp.float32)
        short_im = lax.optimization_barrier(basis_im.astype(jnp.bfloat16)).astype(jnp.float32)
        first_row = jnp.stack([short_re, short_im], -2)
        second_row = jnp.stack([-short_im, short_re], -2)
        mixing = jnp.stack([first_row, second_row], 1)
        fields_out = jnp.einsum('mcbkx,mcbdj->mdjkx', coeffs_wide, mixing)
        factor = lax.rsqrt(energy)[:, None, :, None, None] * jnp.sqrt(weight)
        return ((fields_out * factor).astype(jnp.bfloat16), energy)
    mode_fields, energy = lax.map(one_freq, jnp.arange(NFREQ, dtype=jnp.int32))
    return (jnp.transpose(mode_fields, (1, 0, 2, 3, 4, 5)), jnp.transpose(energy, (1, 0, 2)))
```

```python
import functools

import jax
import jax.numpy as jnp
import ml_dtypes
import numpy as np
from jax import lax
from jax.experimental import pallas as pl
from jax.experimental.pallas import tpu as pltpu
from jax.sharding import PartitionSpec as P

NFFT = 64
NFREQ = 32
MODES = 8
SUBIT = 4
EPSILON = 1e-06
MESH = pl.DeviceIdType.MESH
BF = jnp.bfloat16
F32 = jnp.float32

SECTORS = 16
ORDERS = 8
TMS = 2
SPACE = 4
BLK = 8
BLOCKS = TMS * BLK
FIELDS = 3
TREC = 296
CELLS = 2048
NSLAB = 16
SLOTS = TMS * SECTORS
ROWS = 2 * BLK
LANES = 128
TILE = 512


def time_table():
    t = np.arange(NFFT, dtype=np.float32)
    f = np.arange(NFREQ, dtype=np.float32)
    two_pi = np.float32(2.0 * np.pi)
    window = np.float32(0.5) - np.float32(0.5) * np.cos(two_pi * t / np.float32(NFFT))
    angles = two_pi * f[:, None] * t[None, :] / np.float32(NFFT)
    both = np.stack([window * np.cos(angles), -window * np.sin(angles)])
    return (both / np.float32(np.sqrt(NFFT))).astype(ml_dtypes.bfloat16)


def order_table():
    m = np.arange(ORDERS, dtype=np.float32)[:, None]
    s = np.arange(SECTORS, dtype=np.float32)[None, :]
    angles = np.float32(2.0 * np.pi) * m * s / np.float32(SECTORS)
    cosine, sine = np.cos(angles), np.sin(angles)
    both = np.stack([np.stack([cosine, sine], -1), np.stack([-sine, cosine], -1)], 1)
    return (both / np.float32(np.sqrt(SECTORS))).astype(ml_dtypes.bfloat16)


def spread_time_table():
    basis = time_table().astype(np.float32)
    wide = np.zeros((NFREQ, BLK, 2, BLK, NFFT), np.float32)
    for b in range(BLK):
        wide[:, b, :, b, :] = basis.transpose(1, 0, 2)
    return wide.reshape(NFREQ * ROWS, BLK * NFFT).astype(ml_dtypes.bfloat16)


def spread_order_table():
    table = order_table().astype(np.float32)
    wide = np.zeros((2, ORDERS, TMS, BLK, TMS, SECTORS, BLK, 2), np.float32)
    for j in range(TMS):
        for b in range(BLK):
            wide[:, :, j, b, j, :, b, :] = table.transpose(1, 0, 2, 3)
    return wide.reshape(2 * ORDERS * BLOCKS, SLOTS * ROWS).astype(ml_dtypes.bfloat16)


def place():
    sector, tm, y = lax.axis_index("sector"), lax.axis_index("tm"), lax.axis_index("space")
    return tm * 2 + (sector // 2) % 2, y, sector // 4, sector % 2


def device_at(x, y, z, core):
    return (z * 4 + (x % 2) * 2 + core, x // 2, y)


def send_order():
    dist = (0, 1, 2, 1)
    offsets = [
        (a, b, c) for a in range(4) for b in range(4) for c in range(2) if (a, b, c) != (0, 0, 0)
    ]
    offsets.sort(key=lambda o: -(dist[o[0]] + dist[o[1]]))
    order = []
    for a, b, c in offsets:
        for o in ((a, b, c), (-a % 4, -b % 4, c), (b, a, c), (-b % 4, -a % 4, c)):
            if o not in order:
                order.append(o)
    return order


ORDER = send_order()


def weight_row(slab_ref, table_ref):
    slab = slab_ref[...]
    weight = jnp.zeros(slab.shape, F32)
    for n in range(NSLAB):
        weight = jnp.where(slab == n, table_ref[n], weight)
    return weight


def gather_kernel(
    rec_hbm, start_ref, table_ref, slab_ref, basis_ref, order_ref, coef_hbm, gram_ref,
    rec, send, recv, coef, band, shift, weight, acc, slots,
    rec_sem, own_sem, send_sem, recv_sem, coef_sem, gsend_sem, grecv_sem,
):
    x, y, z, core = place()
    tm = x // 2
    own = tm * SECTORS + z * 4 + (x % 2) * 2 + core

    def peer(offset):
        a, b, c = offset
        return (x + a + core * (b - a)) % 4, y, (z + b + core * (a - b)) % 4, (core + c) % 2

    barrier = pltpu.get_barrier_semaphore()
    for offset in ORDER:
        pl.semaphore_signal(barrier, inc=1, device_id=device_at(*peer(offset)), device_id_type=MESH)
    for d in range(1, SPACE):
        pl.semaphore_signal(
            barrier, inc=1, device_id=device_at(x, (y + d) % SPACE, z, core), device_id_type=MESH
        )
    loads = [
        pltpu.make_async_copy(rec_hbm.at[k], rec.at[k], rec_sem.at[k]) for k in range(FIELDS)
    ]
    for load in loads:
        load.start()

    weight[...] = weight_row(slab_ref, table_ref)
    step = lax.broadcasted_iota(jnp.int32, (NFFT, TREC), 1) - lax.broadcasted_iota(
        jnp.int32, (NFFT, TREC), 0
    )
    for b in range(BLK):
        shift[b * NFFT : (b + 1) * NFFT, :] = jnp.where(
            step == start_ref[tm * BLK + b], 1.0, 0.0
        ).astype(BF)
    band[...] = jnp.dot(basis_ref[...], shift[...], preferred_element_type=F32).astype(BF)

    copies, owns = [], []
    for k in range(FIELDS):
        loads[k].wait()

        @pl.loop(0, CELLS // TILE)
        def _(t):
            cols = pl.ds(pl.multiple_of(t * TILE, TILE), TILE)
            out = jnp.dot(band[...], rec[k, :, cols], preferred_element_type=F32)
            send[k, :, :, cols] = out.astype(BF).reshape(NFREQ, ROWS, TILE)

        if k == 0:
            pl.semaphore_wait(barrier, len(ORDER) + SPACE - 1)
        for i, offset in enumerate(ORDER):
            px, py, pz, pc = peer(offset)
            sector, ptm, _ = device_at(px, py, pz, pc)
            copy = pltpu.make_async_remote_copy(
                src_ref=send.at[k, sector * TMS + ptm],
                dst_ref=recv.at[k, own],
                send_sem=send_sem.at[k, i],
                recv_sem=recv_sem.at[k, i],
                device_id=device_at(px, py, pz, pc),
                device_id_type=MESH,
            )
            copy.start()
            copies.append(copy)
        sector, ptm, _ = device_at(x, y, z, core)
        mine = pltpu.make_async_copy(
            send.at[k, sector * TMS + ptm], recv.at[k, own], own_sem.at[k]
        )
        mine.start()
        owns.append(mine)

    acc[...] = jnp.zeros_like(acc)
    stores = []
    for k in range(FIELDS):
        for copy in copies[k * len(ORDER) : (k + 1) * len(ORDER)]:
            copy.wait_recv()
        owns[k].wait()

        @pl.loop(0, CELLS // TILE)
        def _(t):
            cols = pl.ds(pl.multiple_of(t * TILE, TILE), TILE)
            arrived = recv[k, :, :, cols].reshape(SLOTS * ROWS, TILE)
            c = jnp.dot(order_ref[...], arrived, preferred_element_type=F32).astype(BF)
            coef[k, :, cols] = c
            weighted = (c.astype(F32) * weight[:, cols]).astype(BF)
            acc[...] += lax.dot_general(
                weighted, c, (((1,), (1,)), ((), ())), preferred_element_type=F32
            )

        store = pltpu.make_async_copy(coef.at[k], coef_hbm.at[k], coef_sem.at[k])
        store.start()
        stores.append(store)

    half = ORDERS * BLOCKS
    full_re = acc[:half, :half] + acc[half:, half:]
    full_im = acc[:half, half:] - acc[half:, :half]
    group = lax.broadcasted_iota(jnp.int32, (BLOCKS, half), 1) // BLOCKS
    gram_re = jnp.zeros((BLOCKS, half), F32)
    gram_im = jnp.zeros((BLOCKS, half), F32)
    for m in range(ORDERS):
        rows = slice(m * BLOCKS, (m + 1) * BLOCKS)
        gram_re = jnp.where(group == m, full_re[rows], gram_re)
        gram_im = jnp.where(group == m, full_im[rows], gram_im)
    slots[y, 0] = gram_re
    slots[y, 1] = gram_im
    swaps = []
    for d in range(1, SPACE):
        swap = pltpu.make_async_remote_copy(
            src_ref=slots.at[y],
            dst_ref=slots.at[y],
            send_sem=gsend_sem.at[d - 1],
            recv_sem=grecv_sem.at[d - 1],
            device_id=device_at(x, (y + d) % SPACE, z, core),
            device_id_type=MESH,
        )
        swap.start()
        swaps.append(swap)
    for swap in swaps:
        swap.wait_recv()
    gram_ref[...] = (slots[0] + slots[1]) + (slots[2] + slots[3])
    for swap in swaps:
        swap.wait_send()
    for copy in copies:
        copy.wait_send()
    for store in stores:
        store.wait()


def take(array, index):
    return jnp.take_along_axis(array, index, axis=1)


def modes_kernel(
    coef_hbm, gram_ref, table_ref, slab_ref, out_hbm, energy_ref,
    coef, out, mix, scale, root, coef_sem, out_sem,
):
    loads = [
        pltpu.make_async_copy(coef_hbm.at[k], coef.at[k], coef_sem.at[k]) for k in range(FIELDS)
    ]
    for load in loads:
        load.start()
    root[...] = jnp.sqrt(weight_row(slab_ref, table_ref))

    shape = (BLOCKS, LANES)
    lane = lax.broadcasted_iota(jnp.int32, shape, 1)
    low = lane < LANES // 2
    column = (lane // ORDERS) % MODES
    order = lane % ORDERS
    gram_re, gram_im = gram_ref[0], gram_ref[1]
    both = jnp.concatenate([gram_re, gram_im], 0)
    wide = (BLOCKS * ORDERS, LANES)
    same = (
        lax.broadcasted_iota(jnp.int32, wide, 0) // BLOCKS
        == lax.broadcasted_iota(jnp.int32, wide, 1) % ORDERS
    )

    def apply(re, im):
        right = jnp.where(same, jnp.concatenate([jnp.where(low, re, im)] * ORDERS, 0), 0.0)
        image = jnp.dot(
            both, right, preferred_element_type=F32, precision=lax.Precision.HIGHEST
        )
        turned = pltpu.roll(image, LANES // 2, 1)
        p0, p1, t0, t1 = image[:BLOCKS], image[BLOCKS:], turned[:BLOCKS], turned[BLOCKS:]
        return jnp.where(low, p0 - t1, t0 - p1), jnp.where(low, t0 + p1, p0 + t1)

    def total(a):
        return jnp.sum(a, axis=0, keepdims=True)

    first = order * BLOCKS + column
    re, im = take(gram_re, first), take(gram_im, first)
    for sweep in range(SUBIT):
        if sweep:
            re, im = apply(re, im)
        for i in range(MODES):
            index = order + i * ORDERS
            v_re, v_im = take(re, index), take(im, index)
            size = total(v_re * v_re + v_im * v_im) + EPSILON
            q_re = total(v_re * re + v_im * im) / size
            q_im = total(v_re * im - v_im * re) / size
            norm = lax.rsqrt(size)
            later, here = column > i, column == i
            re, im = (
                jnp.where(
                    later, re - (q_re * v_re - q_im * v_im), jnp.where(here, v_re * norm, re)
                ),
                jnp.where(
                    later, im - (q_re * v_im + q_im * v_re), jnp.where(here, v_im * norm, im)
                ),
            )
    image_re, image_im = apply(re, im)
    energy = total(re * image_re + im * image_im) * (1.0 / (FIELDS * CELLS * SPACE))
    energy = jnp.broadcast_to(energy, shape)

    sub = lax.broadcasted_iota(jnp.int32, (ORDERS, LANES), 0)
    lane8 = lax.broadcasted_iota(jnp.int32, (ORDERS, LANES), 1)
    table = take(energy[:ORDERS], (lane8 % MODES) * ORDERS + sub)
    energy_ref[:, 0, :] = table[:, :MODES]

    target = (lane % MODES) * ORDERS + lane // BLOCKS
    real = (lane // MODES) % 2 == 0
    out_re, out_im = take(re, target), take(im, target)
    diagonal = (
        lax.broadcasted_iota(jnp.int32, wide, 0) // BLOCKS
        == lax.broadcasted_iota(jnp.int32, wide, 1) // BLOCKS
    )
    upper = jnp.where(real, out_re, out_im)
    lower = jnp.where(real, -out_im, out_re)
    for c, part in enumerate((upper, lower)):
        block = jnp.where(diagonal, jnp.concatenate([part] * ORDERS, 0), 0.0)
        mix[:, c * LANES : (c + 1) * LANES] = block.T.astype(BF)
    factor = jnp.broadcast_to(lax.rsqrt(take(energy, target))[:1], (LANES, LANES)).T
    for n in range(TILE // LANES):
        scale[:, n * LANES : (n + 1) * LANES] = factor

    stores = []
    for k in range(FIELDS):
        loads[k].wait()

        @pl.loop(0, CELLS // TILE)
        def _(t):
            cols = pl.ds(pl.multiple_of(t * TILE, TILE), TILE)
            fields = jnp.dot(mix[...], coef[k, :, cols], preferred_element_type=F32)
            fields = fields * (scale[...] * root[:, cols])
            out[:, k, :, cols] = fields.astype(BF).reshape(2 * ORDERS, MODES, TILE)

        store = pltpu.make_async_copy(out.at[:, k], out_hbm.at[:, k], out_sem.at[k])
        store.start()
        stores.append(store)
    for store in stores:
        store.wait()


def local(records, block_start, slab_index, weight_table):
    assert records.shape == (1, TREC, FIELDS, CELLS)
    rec = jnp.transpose(records[0], (1, 0, 2))
    slab = slab_index.reshape(1, CELLS)
    any_spec = pl.BlockSpec(memory_space=pl.ANY)
    smem = pl.BlockSpec(memory_space=pltpu.SMEM)
    vmem = pl.BlockSpec(memory_space=pltpu.VMEM)
    dma = pltpu.SemaphoreType.DMA
    width = 2 * ORDERS * BLOCKS
    count = len(ORDER)
    coef, gram = pl.pallas_call(
        gather_kernel,
        name="gather",
        out_shape=(
            jax.ShapeDtypeStruct((FIELDS, width, CELLS), BF),
            jax.ShapeDtypeStruct((2, BLOCKS, LANES), F32),
        ),
        in_specs=[any_spec, smem, smem, vmem, vmem, vmem],
        out_specs=(any_spec, vmem),
        scratch_shapes=[
            pltpu.VMEM((FIELDS, TREC, CELLS), BF),
            pltpu.VMEM((FIELDS, NFREQ, ROWS, CELLS), BF),
            pltpu.VMEM((FIELDS, SLOTS, ROWS, CELLS), BF),
            pltpu.VMEM((FIELDS, width, CELLS), BF),
            pltpu.VMEM((NFREQ * ROWS, TREC), BF),
            pltpu.VMEM((BLK * NFFT, TREC), BF),
            pltpu.VMEM((1, CELLS), F32),
            pltpu.VMEM((width, width), F32),
            pltpu.VMEM((SPACE, 2, BLOCKS, LANES), F32),
            dma((FIELDS,)),
            dma((FIELDS,)),
            dma((FIELDS, count)),
            dma((FIELDS, count)),
            dma((FIELDS,)),
            dma((SPACE - 1,)),
            dma((SPACE - 1,)),
        ],
        compiler_params=pltpu.CompilerParams(
            collective_id=0, has_side_effects=True, vmem_limit_bytes=48 << 20
        ),
    )(rec, block_start, weight_table, slab, jnp.asarray(spread_time_table()), jnp.asarray(spread_order_table()))
    out, energy = pl.pallas_call(
        modes_kernel,
        name="modes",
        out_shape=(
            jax.ShapeDtypeStruct((2 * ORDERS, FIELDS, MODES, CELLS), BF),
            jax.ShapeDtypeStruct((ORDERS, 1, MODES), F32),
        ),
        in_specs=[any_spec, vmem, smem, vmem],
        out_specs=(any_spec, vmem),
        scratch_shapes=[
            pltpu.VMEM((FIELDS, width, CELLS), BF),
            pltpu.VMEM((2 * ORDERS, FIELDS, MODES, CELLS), BF),
            pltpu.VMEM((LANES, width), BF),
            pltpu.VMEM((LANES, TILE), F32),
            pltpu.VMEM((1, CELLS), F32),
            dma((FIELDS,)),
            dma((FIELDS,)),
        ],
        compiler_params=pltpu.CompilerParams(vmem_limit_bytes=32 << 20),
    )(coef, gram, weight_table, slab)
    out = out.reshape(ORDERS, 1, 2, FIELDS, MODES, CELLS)
    return jnp.transpose(out, (0, 1, 2, 4, 3, 5)), energy


def solution(mesh):
    assert dict(mesh.shape) == {"sector": SECTORS, "tm": TMS, "space": SPACE}
    placed = (P("sector", "tm", None, "space"), P(), P("space"), P())
    return jax.shard_map(
        local,
        mesh=mesh,
        in_specs=placed,
        out_specs=(
            P(None, ("sector", "tm"), None, None, None, "space"),
            P(None, ("sector", "tm"), None),
        ),
        check_vma=False,
    )
```

```python
import functools

import jax
import jax.numpy as jnp
import ml_dtypes
import numpy as np
from jax import lax
from jax.experimental import pallas as pl
from jax.experimental.pallas import tpu as pltpu
from jax.sharding import PartitionSpec as P

NFFT = 64
NFREQ = 32
MODES = 8
SUBIT = 4
EPSILON = 1e-06
MESH = pl.DeviceIdType.MESH
BF = jnp.bfloat16
F32 = jnp.float32

SECTORS = 16
ORDERS = 8
TMS = 2
SPACE = 4
BLK = 8
BLOCKS = TMS * BLK
FIELDS = 3
TREC = 296
CELLS = 2048
NSLAB = 16
SLOTS = TMS * SECTORS
ROWS = 2 * BLK
LANES = 128
TILE = 512
WIDE = 1024
CHUNKS = ((0, 0, 512), (0, 512, 1536), (1, 0, 2048), (2, 0, 1536), (2, 1536, 512))


def time_table():
    t = np.arange(NFFT, dtype=np.float32)
    f = np.arange(NFREQ, dtype=np.float32)
    two_pi = np.float32(2.0 * np.pi)
    window = np.float32(0.5) - np.float32(0.5) * np.cos(two_pi * t / np.float32(NFFT))
    angles = two_pi * f[:, None] * t[None, :] / np.float32(NFFT)
    both = np.stack([window * np.cos(angles), -window * np.sin(angles)])
    return (both / np.float32(np.sqrt(NFFT))).astype(ml_dtypes.bfloat16)


def order_table():
    m = np.arange(ORDERS, dtype=np.float32)[:, None]
    s = np.arange(SECTORS, dtype=np.float32)[None, :]
    angles = np.float32(2.0 * np.pi) * m * s / np.float32(SECTORS)
    cosine, sine = np.cos(angles), np.sin(angles)
    both = np.stack([np.stack([cosine, sine], -1), np.stack([-sine, cosine], -1)], 1)
    return (both / np.float32(np.sqrt(SECTORS))).astype(ml_dtypes.bfloat16)


def spread_time_table():
    basis = time_table().astype(np.float32)
    wide = np.zeros((NFREQ, BLK, 2, BLK, NFFT), np.float32)
    for b in range(BLK):
        wide[:, b, :, b, :] = basis.transpose(1, 0, 2)
    return wide.reshape(NFREQ * ROWS, BLK * NFFT).astype(ml_dtypes.bfloat16)


def spread_order_table():
    table = order_table().astype(np.float32)
    wide = np.zeros((2, ORDERS, TMS, BLK, TMS, SECTORS, BLK, 2), np.float32)
    for j in range(TMS):
        for b in range(BLK):
            wide[:, :, j, b, j, :, b, :] = table.transpose(1, 0, 2, 3)
    return wide.reshape(2 * ORDERS * BLOCKS, SLOTS * ROWS).astype(ml_dtypes.bfloat16)


def place():
    sector, tm, y = lax.axis_index("sector"), lax.axis_index("tm"), lax.axis_index("space")
    return tm * 2 + (sector // 2) % 2, y, sector // 4, sector % 2


def device_at(x, y, z, core):
    return (z * 4 + (x % 2) * 2 + core, x // 2, y)


def send_order():
    dist = (0, 1, 2, 1)
    offsets = [
        (a, b, c) for a in range(4) for b in range(4) for c in range(2) if (a, b, c) != (0, 0, 0)
    ]
    offsets.sort(key=lambda o: -(dist[o[0]] + dist[o[1]]))
    order = []
    for a, b, c in offsets:
        for o in ((a, b, c), (-a % 4, -b % 4, c), (b, a, c), (-b % 4, -a % 4, c)):
            if o not in order:
                order.append(o)
    return order


ORDER = send_order()


def weight_row(slab_ref, table_ref):
    slab = slab_ref[...]
    weight = jnp.zeros(slab.shape, F32)
    for n in range(NSLAB):
        weight = jnp.where(slab == n, table_ref[n], weight)
    return weight


def gather_kernel(
    rec_hbm, start_hbm, table_hbm, slab_hbm, basis_hbm, order_hbm, coef, gram_ref, weight,
    rec, send, recv, start, table, slab, basis, mixer, band, shift, acc, slots,
    in_sem, rec_sem, own_sem, send_sem, recv_sem, gsend_sem, grecv_sem,
):
    x, y, z, core = place()
    tm = x // 2
    own = tm * SECTORS + z * 4 + (x % 2) * 2 + core

    def peer(offset):
        a, b, c = offset
        return (x + a + core * (b - a)) % 4, y, (z + b + core * (a - b)) % 4, (core + c) % 2

    barrier = pltpu.get_barrier_semaphore()
    for offset in ORDER:
        pl.semaphore_signal(barrier, inc=1, device_id=device_at(*peer(offset)), device_id_type=MESH)
    for d in range(1, SPACE):
        pl.semaphore_signal(
            barrier, inc=1, device_id=device_at(x, (y + d) % SPACE, z, core), device_id_type=MESH
        )
    pairs = (
        (start_hbm, start), (basis_hbm, basis), (slab_hbm, slab), (table_hbm, table),
        (order_hbm, mixer),
    )
    smalls = [
        pltpu.make_async_copy(src, dst, in_sem.at[n]) for n, (src, dst) in enumerate(pairs)
    ]
    loads = [
        pltpu.make_async_copy(
            rec_hbm.at[k, :, pl.ds(first, size)], rec.at[k, :, pl.ds(first, size)], rec_sem.at[n]
        )
        for n, (k, first, size) in enumerate(CHUNKS)
    ]
    for load in (smalls[0], smalls[1], loads[0], *loads[1:], *smalls[2:]):
        load.start()
    smalls[0].wait()
    step = lax.broadcasted_iota(jnp.int32, (NFFT, TREC), 1) - lax.broadcasted_iota(
        jnp.int32, (NFFT, TREC), 0
    )
    for b in range(BLK):
        shift[b * NFFT : (b + 1) * NFFT, :] = jnp.where(
            step == start[tm * BLK + b], 1.0, 0.0
        ).astype(BF)
    smalls[1].wait()
    band[...] = jnp.dot(basis[...], shift[...], preferred_element_type=F32).astype(BF)

    copies, owns = [], []
    for n, (k, first, size) in enumerate(CHUNKS):
        loads[n].wait()

        @pl.loop(0, size // TILE)
        def _(t):
            cols = pl.ds(pl.multiple_of(first + t * TILE, TILE), TILE)
            out = jnp.dot(band[...], rec[k, :, cols], preferred_element_type=F32)
            send[k, :, :, cols] = out.astype(BF).reshape(NFREQ, ROWS, TILE)

        if n == 0:
            pl.semaphore_wait(barrier, len(ORDER) + SPACE - 1)
        span = pl.ds(first, size)
        for i, offset in enumerate(ORDER):
            px, py, pz, pc = peer(offset)
            sector, ptm, _ = device_at(px, py, pz, pc)
            copy = pltpu.make_async_remote_copy(
                src_ref=send.at[k, sector * TMS + ptm, :, span],
                dst_ref=recv.at[k, own, :, span],
                send_sem=send_sem.at[n, i],
                recv_sem=recv_sem.at[n, i],
                device_id=device_at(px, py, pz, pc),
                device_id_type=MESH,
            )
            copy.start()
            copies.append(copy)
        sector, ptm, _ = device_at(x, y, z, core)
        mine = pltpu.make_async_copy(
            send.at[k, sector * TMS + ptm, :, span], recv.at[k, own, :, span], own_sem.at[n]
        )
        mine.start()
        owns.append(mine)

    for small in smalls[2:]:
        small.wait()
    weight[...] = weight_row(slab, table)
    acc[...] = jnp.zeros_like(acc)
    for n, (k, first, size) in enumerate(CHUNKS):
        for copy in copies[n * len(ORDER) : (n + 1) * len(ORDER)]:
            copy.wait_recv()
        owns[n].wait()

        @pl.loop(0, size // TILE)
        def _(t):
            cols = pl.ds(pl.multiple_of(first + t * TILE, TILE), TILE)
            arrived = recv[k, :, :, cols].reshape(SLOTS * ROWS, TILE)
            c = jnp.dot(mixer[...], arrived, preferred_element_type=F32).astype(BF)
            coef[k, :, cols] = c
            weighted = (c.astype(F32) * weight[:, cols]).astype(BF)
            acc[...] += lax.dot_general(
                weighted, c, (((1,), (1,)), ((), ())), preferred_element_type=F32
            )

    half = ORDERS * BLOCKS
    full_re = acc[:half, :half] + acc[half:, half:]
    full_im = acc[:half, half:] - acc[half:, :half]
    group = lax.broadcasted_iota(jnp.int32, (BLOCKS, half), 1) // BLOCKS
    gram_re = jnp.zeros((BLOCKS, half), F32)
    gram_im = jnp.zeros((BLOCKS, half), F32)
    for m in range(ORDERS):
        rows = slice(m * BLOCKS, (m + 1) * BLOCKS)
        gram_re = jnp.where(group == m, full_re[rows], gram_re)
        gram_im = jnp.where(group == m, full_im[rows], gram_im)
    slots[y, 0] = gram_re
    slots[y, 1] = gram_im
    swaps = []
    for d in range(1, SPACE):
        swap = pltpu.make_async_remote_copy(
            src_ref=slots.at[y],
            dst_ref=slots.at[y],
            send_sem=gsend_sem.at[d - 1],
            recv_sem=grecv_sem.at[d - 1],
            device_id=device_at(x, (y + d) % SPACE, z, core),
            device_id_type=MESH,
        )
        swap.start()
        swaps.append(swap)
    for swap in swaps:
        swap.wait_recv()
    gram_ref[...] = (slots[0] + slots[1]) + (slots[2] + slots[3])
    for swap in swaps:
        swap.wait_send()
    for copy in copies:
        copy.wait_send()


def take(array, index):
    return jnp.take_along_axis(array, index, axis=1)


def modes_kernel(
    coef, gram_ref, weight, out_hbm, energy_ref, out, mix, scale, root, out_sem,
):
    root[...] = jnp.sqrt(weight[...])

    shape = (BLOCKS, LANES)
    lane = lax.broadcasted_iota(jnp.int32, shape, 1)
    low = lane < LANES // 2
    column = (lane // ORDERS) % MODES
    order = lane % ORDERS
    gram_re, gram_im = gram_ref[0], gram_ref[1]
    both = jnp.concatenate([gram_re, gram_im], 0)
    wide = (BLOCKS * ORDERS, LANES)
    same = (
        lax.broadcasted_iota(jnp.int32, wide, 0) // BLOCKS
        == lax.broadcasted_iota(jnp.int32, wide, 1) % ORDERS
    )

    def apply(re, im):
        right = jnp.where(same, jnp.concatenate([jnp.where(low, re, im)] * ORDERS, 0), 0.0)
        image = jnp.dot(
            both, right, preferred_element_type=F32, precision=lax.Precision.HIGHEST
        )
        turned = pltpu.roll(image, LANES // 2, 1)
        p0, p1, t0, t1 = image[:BLOCKS], image[BLOCKS:], turned[:BLOCKS], turned[BLOCKS:]
        return jnp.where(low, p0 - t1, t0 - p1), jnp.where(low, t0 + p1, p0 + t1)

    def total(a):
        return jnp.sum(a, axis=0, keepdims=True)

    first = order * BLOCKS + column
    re, im = take(gram_re, first), take(gram_im, first)
    for sweep in range(SUBIT):
        if sweep:
            re, im = apply(re, im)
        for i in range(MODES):
            index = order + i * ORDERS
            v_re, v_im = take(re, index), take(im, index)
            norm = lax.rsqrt(total(v_re * v_re + v_im * v_im) + EPSILON)
            inverse = norm * norm
            q_re = total(v_re * re + v_im * im) * inverse
            q_im = total(v_re * im - v_im * re) * inverse
            later, here = column > i, column == i
            re, im = (
                jnp.where(
                    later, re - (q_re * v_re - q_im * v_im), jnp.where(here, v_re * norm, re)
                ),
                jnp.where(
                    later, im - (q_re * v_im + q_im * v_re), jnp.where(here, v_im * norm, im)
                ),
            )
    image_re, image_im = apply(re, im)
    energy = total(re * image_re + im * image_im) * (1.0 / (FIELDS * CELLS * SPACE))
    energy = jnp.broadcast_to(energy, shape)

    sub = lax.broadcasted_iota(jnp.int32, (ORDERS, LANES), 0)
    lane8 = lax.broadcasted_iota(jnp.int32, (ORDERS, LANES), 1)
    table = take(energy[:ORDERS], (lane8 % MODES) * ORDERS + sub)
    energy_ref[:, 0, :] = table[:, :MODES]

    target = (lane % MODES) * ORDERS + lane // BLOCKS
    real = (lane // MODES) % 2 == 0
    out_re, out_im = take(re, target), take(im, target)
    diagonal = (
        lax.broadcasted_iota(jnp.int32, wide, 0) // BLOCKS
        == lax.broadcasted_iota(jnp.int32, wide, 1) // BLOCKS
    )
    upper = jnp.where(real, out_re, out_im)
    lower = jnp.where(real, -out_im, out_re)
    for c, part in enumerate((upper, lower)):
        block = jnp.where(diagonal, jnp.concatenate([part] * ORDERS, 0), 0.0)
        mix[:, c * LANES : (c + 1) * LANES] = block.T.astype(BF)
    factor = jnp.broadcast_to(lax.rsqrt(take(energy, target))[:1], (LANES, LANES)).T
    for n in range(WIDE // LANES):
        scale[:, n * LANES : (n + 1) * LANES] = factor

    stores = []
    for k in range(FIELDS):

        @pl.loop(0, CELLS // WIDE)
        def _(t):
            cols = pl.ds(pl.multiple_of(t * WIDE, WIDE), WIDE)
            fields = jnp.dot(mix[...], coef[k, :, cols], preferred_element_type=F32)
            fields = fields * (scale[...] * root[:, cols])
            out[:, k, :, cols] = fields.astype(BF).reshape(2 * ORDERS, MODES, WIDE)

        store = pltpu.make_async_copy(out.at[:, k], out_hbm.at[:, k], out_sem.at[k])
        store.start()
        stores.append(store)
    for store in stores:
        store.wait()


def local(records, block_start, slab_index, weight_table):
    assert records.shape == (1, TREC, FIELDS, CELLS)
    rec = jnp.transpose(records[0], (1, 0, 2))
    slab = slab_index.reshape(1, CELLS)
    hbm = pl.BlockSpec(memory_space=pltpu.HBM)
    vmem = pl.BlockSpec(memory_space=pltpu.VMEM)
    dma = pltpu.SemaphoreType.DMA
    width = 2 * ORDERS * BLOCKS
    count, chunks = len(ORDER), len(CHUNKS)
    basis, mixer = spread_time_table(), spread_order_table()
    coef, gram, weight = pl.pallas_call(
        gather_kernel,
        name="gather",
        out_shape=(
            jax.ShapeDtypeStruct((FIELDS, width, CELLS), BF),
            jax.ShapeDtypeStruct((2, BLOCKS, LANES), F32),
            jax.ShapeDtypeStruct((1, CELLS), F32),
        ),
        in_specs=[hbm] * 6,
        out_specs=(vmem, vmem, vmem),
        scratch_shapes=[
            pltpu.VMEM((FIELDS, TREC, CELLS), BF),
            pltpu.VMEM((FIELDS, NFREQ, ROWS, CELLS), BF),
            pltpu.VMEM((FIELDS, SLOTS, ROWS, CELLS), BF),
            pltpu.SMEM((BLOCKS,), jnp.int32),
            pltpu.SMEM((NSLAB,), F32),
            pltpu.VMEM((1, CELLS), jnp.int32),
            pltpu.VMEM(basis.shape, BF),
            pltpu.VMEM(mixer.shape, BF),
            pltpu.VMEM((NFREQ * ROWS, TREC), BF),
            pltpu.VMEM((BLK * NFFT, TREC), BF),
            pltpu.VMEM((width, width), F32),
            pltpu.VMEM((SPACE, 2, BLOCKS, LANES), F32),
            dma((5,)),
            dma((chunks,)),
            dma((chunks,)),
            dma((chunks, count)),
            dma((chunks, count)),
            dma((SPACE - 1,)),
            dma((SPACE - 1,)),
        ],
        compiler_params=pltpu.CompilerParams(
            collective_id=0, has_side_effects=True, vmem_limit_bytes=40 << 20
        ),
    )(*(
        pltpu.with_memory_space_constraint(a, pltpu.HBM)
        for a in (rec, block_start, weight_table, slab, jnp.asarray(basis), jnp.asarray(mixer))
    ))
    out, energy = pl.pallas_call(
        modes_kernel,
        name="modes",
        out_shape=(
            jax.ShapeDtypeStruct((2 * ORDERS, FIELDS, MODES, CELLS), BF),
            jax.ShapeDtypeStruct((ORDERS, 1, MODES), F32),
        ),
        in_specs=[vmem, vmem, vmem],
        out_specs=(hbm, vmem),
        scratch_shapes=[
            pltpu.VMEM((2 * ORDERS, FIELDS, MODES, CELLS), BF),
            pltpu.VMEM((LANES, width), BF),
            pltpu.VMEM((LANES, WIDE), F32),
            pltpu.VMEM((1, CELLS), F32),
            dma((FIELDS,)),
        ],
        compiler_params=pltpu.CompilerParams(vmem_limit_bytes=24 << 20),
    )(coef, gram, weight)
    out = out.reshape(ORDERS, 1, 2, FIELDS, MODES, CELLS)
    return jnp.transpose(out, (0, 1, 2, 4, 3, 5)), energy


def solution(mesh):
    assert dict(mesh.shape) == {"sector": SECTORS, "tm": TMS, "space": SPACE}
    placed = (P("sector", "tm", None, "space"), P(), P("space"), P())
    return jax.shard_map(
        local,
        mesh=mesh,
        in_specs=placed,
        out_specs=(
            P(None, ("sector", "tm"), None, None, None, "space"),
            P(None, ("sector", "tm"), None),
        ),
        check_vma=False,
    )
```

```python
import functools

import jax
import jax.numpy as jnp
import ml_dtypes
import numpy as np
from jax import lax
from jax.experimental import pallas as pl
from jax.experimental.pallas import tpu as pltpu
from jax.sharding import PartitionSpec as P

NFFT = 64
NFREQ = 32
MODES = 8
SUBIT = 4
EPSILON = 1e-06
MESH = pl.DeviceIdType.MESH
BF = jnp.bfloat16
F32 = jnp.float32

SECTORS = 16
ORDERS = 8
TMS = 2
SPACE = 4
BLK = 8
BLOCKS = TMS * BLK
FIELDS = 3
TREC = 296
CELLS = 2048
NSLAB = 16
SLOTS = TMS * SECTORS
ROWS = 2 * BLK
LANES = 128
TILE = 512
WIDE = 2048
CHUNKS = ((0, 0, 512), (0, 512, 1536), (1, 0, 2048), (2, 0, 1536), (2, 1536, 512))


def time_table():
    t = np.arange(NFFT, dtype=np.float32)
    f = np.arange(NFREQ, dtype=np.float32)
    two_pi = np.float32(2.0 * np.pi)
    window = np.float32(0.5) - np.float32(0.5) * np.cos(two_pi * t / np.float32(NFFT))
    angles = two_pi * f[:, None] * t[None, :] / np.float32(NFFT)
    both = np.stack([window * np.cos(angles), -window * np.sin(angles)])
    return (both / np.float32(np.sqrt(NFFT))).astype(ml_dtypes.bfloat16)


def order_table():
    m = np.arange(ORDERS, dtype=np.float32)[:, None]
    s = np.arange(SECTORS, dtype=np.float32)[None, :]
    angles = np.float32(2.0 * np.pi) * m * s / np.float32(SECTORS)
    cosine, sine = np.cos(angles), np.sin(angles)
    both = np.stack([np.stack([cosine, sine], -1), np.stack([-sine, cosine], -1)], 1)
    return (both / np.float32(np.sqrt(SECTORS))).astype(ml_dtypes.bfloat16)


def spread_time_table():
    basis = time_table().astype(np.float32)
    wide = np.zeros((NFREQ, BLK, 2, BLK, NFFT), np.float32)
    for b in range(BLK):
        wide[:, b, :, b, :] = basis.transpose(1, 0, 2)
    return wide.reshape(NFREQ * ROWS, BLK * NFFT).astype(ml_dtypes.bfloat16)


def spread_order_table():
    table = order_table().astype(np.float32)
    wide = np.zeros((2, ORDERS, TMS, BLK, TMS, SECTORS, BLK, 2), np.float32)
    for j in range(TMS):
        for b in range(BLK):
            wide[:, :, j, b, j, :, b, :] = table.transpose(1, 0, 2, 3)
    return wide.reshape(2 * ORDERS * BLOCKS, SLOTS * ROWS).astype(ml_dtypes.bfloat16)


def place():
    sector, tm, y = lax.axis_index("sector"), lax.axis_index("tm"), lax.axis_index("space")
    return tm * 2 + (sector // 2) % 2, y, sector // 4, sector % 2


def device_at(x, y, z, core):
    return (z * 4 + (x % 2) * 2 + core, x // 2, y)


def send_order():
    dist = (0, 1, 2, 1)
    offsets = [
        (a, b, c) for a in range(4) for b in range(4) for c in range(2) if (a, b, c) != (0, 0, 0)
    ]
    offsets.sort(key=lambda o: -(dist[o[0]] + dist[o[1]]))
    order = []
    for a, b, c in offsets:
        for o in ((a, b, c), (-a % 4, -b % 4, c), (b, a, c), (-b % 4, -a % 4, c)):
            if o not in order:
                order.append(o)
    return order


ORDER = send_order()


def weight_row(slab_ref, table_ref):
    slab = slab_ref[...]
    weight = jnp.zeros(slab.shape, F32)
    for n in range(NSLAB):
        weight = jnp.where(slab == n, table_ref[n], weight)
    return weight


def gather_kernel(
    rec_hbm, start_hbm, table_hbm, slab_hbm, basis_hbm, order_hbm, coef, gram_ref, weight,
    rec, send, recv, start, table, slab, basis, mixer, band, shift, acc, slots,
    in_sem, rec_sem, own_sem, send_sem, recv_sem, gsend_sem, grecv_sem,
):
    x, y, z, core = place()
    tm = x // 2
    own = tm * SECTORS + z * 4 + (x % 2) * 2 + core

    def peer(offset):
        a, b, c = offset
        return (x + a + core * (b - a)) % 4, y, (z + b + core * (a - b)) % 4, (core + c) % 2

    barrier = pltpu.get_barrier_semaphore()
    for offset in ORDER:
        pl.semaphore_signal(barrier, inc=1, device_id=device_at(*peer(offset)), device_id_type=MESH)
    for d in range(1, SPACE):
        pl.semaphore_signal(
            barrier, inc=1, device_id=device_at(x, (y + d) % SPACE, z, core), device_id_type=MESH
        )
    pairs = (
        (start_hbm, start), (basis_hbm, basis), (slab_hbm, slab), (table_hbm, table),
        (order_hbm, mixer),
    )
    smalls = [
        pltpu.make_async_copy(src, dst, in_sem.at[n]) for n, (src, dst) in enumerate(pairs)
    ]
    loads = [
        pltpu.make_async_copy(
            rec_hbm.at[k, :, pl.ds(first, size)], rec.at[k, :, pl.ds(first, size)], rec_sem.at[n]
        )
        for n, (k, first, size) in enumerate(CHUNKS)
    ]
    for load in (smalls[0], smalls[1], loads[0], *loads[1:], *smalls[2:]):
        load.start()
    smalls[0].wait()
    step = lax.broadcasted_iota(jnp.int32, (NFFT, TREC), 1) - lax.broadcasted_iota(
        jnp.int32, (NFFT, TREC), 0
    )
    for b in range(BLK):
        shift[b * NFFT : (b + 1) * NFFT, :] = jnp.where(
            step == start[tm * BLK + b], 1.0, 0.0
        ).astype(BF)
    smalls[1].wait()
    band[...] = jnp.dot(basis[...], shift[...], preferred_element_type=F32).astype(BF)

    copies, owns = [], []
    for n, (k, first, size) in enumerate(CHUNKS):
        loads[n].wait()

        @pl.loop(0, size // TILE)
        def _(t):
            cols = pl.ds(pl.multiple_of(first + t * TILE, TILE), TILE)
            out = jnp.dot(band[...], rec[k, :, cols], preferred_element_type=F32)
            send[k, :, :, cols] = out.astype(BF).reshape(NFREQ, ROWS, TILE)

        if n == 0:
            pl.semaphore_wait(barrier, len(ORDER) + SPACE - 1)
        span = pl.ds(first, size)
        for i, offset in enumerate(ORDER):
            px, py, pz, pc = peer(offset)
            sector, ptm, _ = device_at(px, py, pz, pc)
            copy = pltpu.make_async_remote_copy(
                src_ref=send.at[k, sector * TMS + ptm, :, span],
                dst_ref=recv.at[k, own, :, span],
                send_sem=send_sem.at[n, i],
                recv_sem=recv_sem.at[n, i],
                device_id=device_at(px, py, pz, pc),
                device_id_type=MESH,
            )
            copy.start()
            copies.append(copy)
        sector, ptm, _ = device_at(x, y, z, core)
        mine = pltpu.make_async_copy(
            send.at[k, sector * TMS + ptm, :, span], recv.at[k, own, :, span], own_sem.at[n]
        )
        mine.start()
        owns.append(mine)

    for small in smalls[2:]:
        small.wait()
    weight[...] = weight_row(slab, table)
    acc[...] = jnp.zeros_like(acc)
    for n, (k, first, size) in enumerate(CHUNKS):
        for copy in copies[n * len(ORDER) : (n + 1) * len(ORDER)]:
            copy.wait_recv()
        owns[n].wait()

        @pl.loop(0, size // TILE)
        def _(t):
            cols = pl.ds(pl.multiple_of(first + t * TILE, TILE), TILE)
            arrived = recv[k, :, :, cols].reshape(SLOTS * ROWS, TILE)
            c = jnp.dot(mixer[...], arrived, preferred_element_type=F32).astype(BF)
            coef[k, :, cols] = c
            weighted = (c.astype(F32) * weight[:, cols]).astype(BF)
            acc[...] += lax.dot_general(
                weighted, c, (((1,), (1,)), ((), ())), preferred_element_type=F32
            )

    half = ORDERS * BLOCKS
    full_re = acc[:half, :half] + acc[half:, half:]
    full_im = acc[:half, half:] - acc[half:, :half]
    group = lax.broadcasted_iota(jnp.int32, (BLOCKS, half), 1) // BLOCKS
    gram_re = jnp.zeros((BLOCKS, half), F32)
    gram_im = jnp.zeros((BLOCKS, half), F32)
    for m in range(ORDERS):
        rows = slice(m * BLOCKS, (m + 1) * BLOCKS)
        gram_re = jnp.where(group == m, full_re[rows], gram_re)
        gram_im = jnp.where(group == m, full_im[rows], gram_im)
    slots[y, 0] = gram_re
    slots[y, 1] = gram_im
    swaps = []
    for d in range(1, SPACE):
        swap = pltpu.make_async_remote_copy(
            src_ref=slots.at[y],
            dst_ref=slots.at[y],
            send_sem=gsend_sem.at[d - 1],
            recv_sem=grecv_sem.at[d - 1],
            device_id=device_at(x, (y + d) % SPACE, z, core),
            device_id_type=MESH,
        )
        swap.start()
        swaps.append(swap)
    for swap in swaps:
        swap.wait_recv()
    gram_ref[...] = (slots[0] + slots[1]) + (slots[2] + slots[3])
    for swap in swaps:
        swap.wait_send()
    for copy in copies:
        copy.wait_send()


def take(array, index):
    return jnp.take_along_axis(array, index, axis=1)


def modes_kernel(
    coef, gram_ref, weight, out_hbm, energy_ref, out, mix, scale, root, out_sem,
):
    root[...] = jnp.sqrt(weight[...])

    shape = (BLOCKS, LANES)
    lane = lax.broadcasted_iota(jnp.int32, shape, 1)
    column = (lane // ORDERS) % MODES
    order = lane % ORDERS
    gram_re, gram_im = gram_ref[0], gram_ref[1]
    wide = (BLOCKS * ORDERS, LANES)
    grid = [
        (take(gram_re, order * BLOCKS + e), take(gram_im, order * BLOCKS + e))
        for e in range(BLOCKS)
    ]

    def added(terms):
        while len(terms) > 1:
            terms = [sum(terms[n : n + 2]) for n in range(0, len(terms), 2)]
        return terms[0]

    def apply(re, im):
        parts = [
            (g_re, g_im, re[e : e + 1], im[e : e + 1]) for e, (g_re, g_im) in enumerate(grid)
        ]
        return (
            added([g_re * v_re - g_im * v_im for g_re, g_im, v_re, v_im in parts]),
            added([g_re * v_im + g_im * v_re for g_re, g_im, v_re, v_im in parts]),
        )

    def total(a):
        return jnp.sum(a, axis=0, keepdims=True)

    first = order * BLOCKS + column
    re, im = take(gram_re, first), take(gram_im, first)
    for sweep in range(SUBIT):
        if sweep:
            re, im = apply(re, im)
        columns = [
            (take(re, order + i * ORDERS), take(im, order + i * ORDERS)) for i in range(MODES)
        ]
        for i in range(MODES):
            v_re, v_im = columns[i]
            norm = lax.rsqrt(total(v_re * v_re + v_im * v_im) + EPSILON)
            inverse = norm * norm
            for j in range(i + 1, MODES):
                u_re, u_im = columns[j]
                q_re = total(v_re * u_re + v_im * u_im) * inverse
                q_im = total(v_re * u_im - v_im * u_re) * inverse
                columns[j] = (
                    u_re - (q_re * v_re - q_im * v_im), u_im - (q_re * v_im + q_im * v_re)
                )
            columns[i] = v_re * norm, v_im * norm
        re, im = columns[0]
        for i in range(1, MODES):
            re, im = (
                jnp.where(column == i, columns[i][0], re), jnp.where(column == i, columns[i][1], im)
            )
    image_re, image_im = apply(re, im)
    energy = total(re * image_re + im * image_im) * (1.0 / (FIELDS * CELLS * SPACE))
    energy = jnp.broadcast_to(energy, shape)

    sub = lax.broadcasted_iota(jnp.int32, (ORDERS, LANES), 0)
    lane8 = lax.broadcasted_iota(jnp.int32, (ORDERS, LANES), 1)
    table = take(energy[:ORDERS], (lane8 % MODES) * ORDERS + sub)
    energy_ref[:, 0, :] = table[:, :MODES]

    target = (lane % MODES) * ORDERS + lane // BLOCKS
    real = (lane // MODES) % 2 == 0
    out_re, out_im = take(re, target), take(im, target)
    diagonal = (
        lax.broadcasted_iota(jnp.int32, wide, 0) // BLOCKS
        == lax.broadcasted_iota(jnp.int32, wide, 1) // BLOCKS
    )
    upper = jnp.where(real, out_re, out_im)
    lower = jnp.where(real, -out_im, out_re)
    for c, part in enumerate((upper, lower)):
        block = jnp.where(diagonal, jnp.concatenate([part] * ORDERS, 0), 0.0)
        mix[:, c * LANES : (c + 1) * LANES] = block.T.astype(BF)
    factor = jnp.broadcast_to(lax.rsqrt(take(energy, target))[:1], (LANES, LANES)).T
    for n in range(WIDE // LANES):
        scale[:, n * LANES : (n + 1) * LANES] = factor

    stores = []
    for k in range(FIELDS):

        @pl.loop(0, CELLS // WIDE)
        def _(t):
            cols = pl.ds(pl.multiple_of(t * WIDE, WIDE), WIDE)
            fields = jnp.dot(mix[...], coef[k, :, cols], preferred_element_type=F32)
            fields = fields * (scale[...] * root[:, cols])
            out[:, k, :, cols] = fields.astype(BF).reshape(2 * ORDERS, MODES, WIDE)

        store = pltpu.make_async_copy(out.at[:, k], out_hbm.at[:, k], out_sem.at[k])
        store.start()
        stores.append(store)
    for store in stores:
        store.wait()


def local(records, block_start, slab_index, weight_table):
    assert records.shape == (1, TREC, FIELDS, CELLS)
    rec = jnp.transpose(records[0], (1, 0, 2))
    slab = slab_index.reshape(1, CELLS)
    hbm = pl.BlockSpec(memory_space=pltpu.HBM)
    vmem = pl.BlockSpec(memory_space=pltpu.VMEM)
    dma = pltpu.SemaphoreType.DMA
    width = 2 * ORDERS * BLOCKS
    count, chunks = len(ORDER), len(CHUNKS)
    basis, mixer = spread_time_table(), spread_order_table()
    coef, gram, weight = pl.pallas_call(
        gather_kernel,
        name="gather",
        out_shape=(
            jax.ShapeDtypeStruct((FIELDS, width, CELLS), BF),
            jax.ShapeDtypeStruct((2, BLOCKS, LANES), F32),
            jax.ShapeDtypeStruct((1, CELLS), F32),
        ),
        in_specs=[hbm] * 6,
        out_specs=(vmem, vmem, vmem),
        scratch_shapes=[
            pltpu.VMEM((FIELDS, TREC, CELLS), BF),
            pltpu.VMEM((FIELDS, NFREQ, ROWS, CELLS), BF),
            pltpu.VMEM((FIELDS, SLOTS, ROWS, CELLS), BF),
            pltpu.SMEM((BLOCKS,), jnp.int32),
            pltpu.SMEM((NSLAB,), F32),
            pltpu.VMEM((1, CELLS), jnp.int32),
            pltpu.VMEM(basis.shape, BF),
            pltpu.VMEM(mixer.shape, BF),
            pltpu.VMEM((NFREQ * ROWS, TREC), BF),
            pltpu.VMEM((BLK * NFFT, TREC), BF),
            pltpu.VMEM((width, width), F32),
            pltpu.VMEM((SPACE, 2, BLOCKS, LANES), F32),
            dma((5,)),
            dma((chunks,)),
            dma((chunks,)),
            dma((chunks, count)),
            dma((chunks, count)),
            dma((SPACE - 1,)),
            dma((SPACE - 1,)),
        ],
        compiler_params=pltpu.CompilerParams(
            collective_id=0, has_side_effects=True, vmem_limit_bytes=40 << 20
        ),
    )(*(
        pltpu.with_memory_space_constraint(a, pltpu.HBM)
        for a in (rec, block_start, weight_table, slab, jnp.asarray(basis), jnp.asarray(mixer))
    ))
    out, energy = pl.pallas_call(
        modes_kernel,
        name="modes",
        out_shape=(
            jax.ShapeDtypeStruct((2 * ORDERS, FIELDS, MODES, CELLS), BF),
            jax.ShapeDtypeStruct((ORDERS, 1, MODES), F32),
        ),
        in_specs=[vmem, vmem, vmem],
        out_specs=(hbm, vmem),
        scratch_shapes=[
            pltpu.VMEM((2 * ORDERS, FIELDS, MODES, CELLS), BF),
            pltpu.VMEM((LANES, width), BF),
            pltpu.VMEM((LANES, WIDE), F32),
            pltpu.VMEM((1, CELLS), F32),
            dma((FIELDS,)),
        ],
        compiler_params=pltpu.CompilerParams(vmem_limit_bytes=24 << 20),
    )(coef, gram, weight)
    out = out.reshape(ORDERS, 1, 2, FIELDS, MODES, CELLS)
    return jnp.transpose(out, (0, 1, 2, 4, 3, 5)), energy


def solution(mesh):
    assert dict(mesh.shape) == {"sector": SECTORS, "tm": TMS, "space": SPACE}
    placed = (P("sector", "tm", None, "space"), P(), P("space"), P())
    return jax.shard_map(
        local,
        mesh=mesh,
        in_specs=placed,
        out_specs=(
            P(None, ("sector", "tm"), None, None, None, "space"),
            P(None, ("sector", "tm"), None),
        ),
        check_vma=False,
    )
```

```python
import functools

import jax
import jax.numpy as jnp
import ml_dtypes
import numpy as np
from jax import lax
from jax.experimental import pallas as pl
from jax.experimental.pallas import tpu as pltpu
from jax.sharding import PartitionSpec as P

NFFT = 64
NFREQ = 32
MODES = 8
SUBIT = 4
EPSILON = 1e-06
MESH = pl.DeviceIdType.MESH
BF = jnp.bfloat16
F32 = jnp.float32

SECTORS = 16
ORDERS = 8
TMS = 2
SPACE = 4
BLK = 8
BLOCKS = TMS * BLK
FIELDS = 3
TREC = 296
CELLS = 2048
NSLAB = 16
SLOTS = TMS * SECTORS
ROWS = 2 * BLK
LANES = 128
WIDE = 2048
CHUNKS = ((0, 0, 2048), (1, 0, 2048), (2, 0, 2048))


def time_table():
    t = np.arange(NFFT, dtype=np.float32)
    f = np.arange(NFREQ, dtype=np.float32)
    two_pi = np.float32(2.0 * np.pi)
    window = np.float32(0.5) - np.float32(0.5) * np.cos(two_pi * t / np.float32(NFFT))
    angles = two_pi * f[:, None] * t[None, :] / np.float32(NFFT)
    both = np.stack([window * np.cos(angles), -window * np.sin(angles)])
    return (both / np.float32(np.sqrt(NFFT))).astype(ml_dtypes.bfloat16)


def order_table():
    m = np.arange(ORDERS, dtype=np.float32)[:, None]
    s = np.arange(SECTORS, dtype=np.float32)[None, :]
    angles = np.float32(2.0 * np.pi) * m * s / np.float32(SECTORS)
    cosine, sine = np.cos(angles), np.sin(angles)
    both = np.stack([np.stack([cosine, sine], -1), np.stack([-sine, cosine], -1)], 1)
    return (both / np.float32(np.sqrt(SECTORS))).astype(ml_dtypes.bfloat16)


def spread_time_table():
    basis = time_table().astype(np.float32)
    wide = np.zeros((NFREQ, BLK, 2, BLK, NFFT), np.float32)
    for b in range(BLK):
        wide[:, b, :, b, :] = basis.transpose(1, 0, 2)
    return wide.reshape(NFREQ * ROWS, BLK * NFFT).astype(ml_dtypes.bfloat16)


def spread_order_table():
    table = order_table().astype(np.float32)
    wide = np.zeros((2, ORDERS, TMS, BLK, TMS, SECTORS, BLK, 2), np.float32)
    for j in range(TMS):
        for b in range(BLK):
            wide[:, :, j, b, j, :, b, :] = table.transpose(1, 0, 2, 3)
    return wide.reshape(2 * ORDERS * BLOCKS, SLOTS * ROWS).astype(ml_dtypes.bfloat16)


def place():
    sector, tm, y = lax.axis_index("sector"), lax.axis_index("tm"), lax.axis_index("space")
    return tm * 2 + (sector // 2) % 2, y, sector // 4, sector % 2


def device_at(x, y, z, core):
    return (z * 4 + (x % 2) * 2 + core, x // 2, y)


def send_order():
    dist = (0, 1, 2, 1)
    offsets = [
        (a, b, c) for a in range(4) for b in range(4) for c in range(2) if (a, b, c) != (0, 0, 0)
    ]
    offsets.sort(key=lambda o: -(dist[o[0]] + dist[o[1]]))
    order = []
    for a, b, c in offsets:
        for o in ((a, b, c), (-a % 4, -b % 4, c), (b, a, c), (-b % 4, -a % 4, c)):
            if o not in order:
                order.append(o)
    return order


ORDER = send_order()


def weight_row(slab_ref, table_ref):
    slab = slab_ref[...]
    weight = jnp.zeros(slab.shape, F32)
    for n in range(NSLAB):
        weight = jnp.where(slab == n, table_ref[n], weight)
    return weight


def gather_kernel(
    rec_hbm, start_hbm, table_hbm, slab_hbm, basis_hbm, order_hbm, coef, gram_ref, weight,
    rec, send, recv, start, table, slab, basis, mixer, band, shift, acc, slots,
    in_sem, rec_sem, own_sem, send_sem, recv_sem, gsend_sem, grecv_sem,
):
    x, y, z, core = place()
    tm = x // 2
    own = tm * SECTORS + z * 4 + (x % 2) * 2 + core

    def peer(offset):
        a, b, c = offset
        return (x + a + core * (b - a)) % 4, y, (z + b + core * (a - b)) % 4, (core + c) % 2

    barrier = pltpu.get_barrier_semaphore()
    for offset in ORDER:
        pl.semaphore_signal(barrier, inc=1, device_id=device_at(*peer(offset)), device_id_type=MESH)
    for d in range(1, SPACE):
        pl.semaphore_signal(
            barrier, inc=1, device_id=device_at(x, (y + d) % SPACE, z, core), device_id_type=MESH
        )
    pairs = (
        (start_hbm, start), (basis_hbm, basis), (slab_hbm, slab), (table_hbm, table),
        (order_hbm, mixer),
    )
    smalls = [
        pltpu.make_async_copy(src, dst, in_sem.at[n]) for n, (src, dst) in enumerate(pairs)
    ]
    loads = [
        pltpu.make_async_copy(
            rec_hbm.at[k, :, pl.ds(first, size)], rec.at[k, :, pl.ds(first, size)], rec_sem.at[n]
        )
        for n, (k, first, size) in enumerate(CHUNKS)
    ]
    for load in (smalls[0], smalls[1], loads[0], *loads[1:], *smalls[2:]):
        load.start()
    smalls[0].wait()
    step = lax.broadcasted_iota(jnp.int32, (NFFT, TREC), 1) - lax.broadcasted_iota(
        jnp.int32, (NFFT, TREC), 0
    )
    for b in range(BLK):
        shift[b * NFFT : (b + 1) * NFFT, :] = jnp.where(
            step == start[tm * BLK + b], 1.0, 0.0
        ).astype(BF)
    smalls[1].wait()
    band[...] = jnp.dot(basis[...], shift[...], preferred_element_type=F32).astype(BF)

    copies, owns = [], []
    for n, (k, first, size) in enumerate(CHUNKS):
        loads[n].wait()
        span = pl.ds(first, size)
        out = jnp.dot(band[...], rec[k, :, span], preferred_element_type=F32)
        send[k, :, :, span] = out.astype(BF).reshape(NFREQ, ROWS, size)

        if n == 0:
            pl.semaphore_wait(barrier, len(ORDER) + SPACE - 1)
        for i, offset in enumerate(ORDER):
            px, py, pz, pc = peer(offset)
            sector, ptm, _ = device_at(px, py, pz, pc)
            copy = pltpu.make_async_remote_copy(
                src_ref=send.at[k, sector * TMS + ptm, :, span],
                dst_ref=recv.at[k, own, :, span],
                send_sem=send_sem.at[n, i],
                recv_sem=recv_sem.at[n, i],
                device_id=device_at(px, py, pz, pc),
                device_id_type=MESH,
            )
            copy.start()
            copies.append(copy)
        sector, ptm, _ = device_at(x, y, z, core)
        mine = pltpu.make_async_copy(
            send.at[k, sector * TMS + ptm, :, span], recv.at[k, own, :, span], own_sem.at[n]
        )
        mine.start()
        owns.append(mine)

    for small in smalls[2:]:
        small.wait()
    weight[...] = weight_row(slab, table)
    acc[...] = jnp.zeros_like(acc)
    for n, (k, first, size) in enumerate(CHUNKS):
        for copy in copies[n * len(ORDER) : (n + 1) * len(ORDER)]:
            copy.wait_recv()
        owns[n].wait()
        span = pl.ds(first, size)
        arrived = recv[k, :, :, span].reshape(SLOTS * ROWS, size)
        c = jnp.dot(mixer[...], arrived, preferred_element_type=F32).astype(BF)
        coef[k, :, span] = c
        weighted = (c.astype(F32) * weight[:, span]).astype(BF)
        acc[...] += lax.dot_general(
            weighted, c, (((1,), (1,)), ((), ())), preferred_element_type=F32
        )

    half = ORDERS * BLOCKS
    full_re = acc[:half, :half] + acc[half:, half:]
    full_im = acc[:half, half:] - acc[half:, :half]
    group = lax.broadcasted_iota(jnp.int32, (BLOCKS, half), 1) // BLOCKS
    gram_re = jnp.zeros((BLOCKS, half), F32)
    gram_im = jnp.zeros((BLOCKS, half), F32)
    for m in range(ORDERS):
        rows = slice(m * BLOCKS, (m + 1) * BLOCKS)
        gram_re = jnp.where(group == m, full_re[rows], gram_re)
        gram_im = jnp.where(group == m, full_im[rows], gram_im)
    slots[y, 0] = gram_re
    slots[y, 1] = gram_im
    swaps = []
    for d in range(1, SPACE):
        swap = pltpu.make_async_remote_copy(
            src_ref=slots.at[y],
            dst_ref=slots.at[y],
            send_sem=gsend_sem.at[d - 1],
            recv_sem=grecv_sem.at[d - 1],
            device_id=device_at(x, (y + d) % SPACE, z, core),
            device_id_type=MESH,
        )
        swap.start()
        swaps.append(swap)
    for copy in copies:
        copy.wait_send()
    for swap in swaps:
        swap.wait_recv()
    gram_ref[...] = (slots[0] + slots[1]) + (slots[2] + slots[3])
    for swap in swaps:
        swap.wait_send()


def take(array, index):
    return jnp.take_along_axis(array, index, axis=1)


def modes_kernel(
    coef, gram_ref, weight, out_hbm, energy_ref, out, mix, scale, root, out_sem,
):
    root[...] = jnp.sqrt(weight[...])

    shape = (BLOCKS, LANES)
    lane = lax.broadcasted_iota(jnp.int32, shape, 1)
    column = (lane // ORDERS) % MODES
    order = lane % ORDERS
    gram_re, gram_im = gram_ref[0], gram_ref[1]
    wide = (BLOCKS * ORDERS, LANES)
    grid = [
        (take(gram_re, order * BLOCKS + e), take(gram_im, order * BLOCKS + e))
        for e in range(BLOCKS)
    ]

    def added(terms):
        while len(terms) > 1:
            terms = [sum(terms[n : n + 2]) for n in range(0, len(terms), 2)]
        return terms[0]

    def apply(re, im):
        parts = [
            (g_re, g_im, re[e : e + 1], im[e : e + 1]) for e, (g_re, g_im) in enumerate(grid)
        ]
        return (
            added([g_re * v_re - g_im * v_im for g_re, g_im, v_re, v_im in parts]),
            added([g_re * v_im + g_im * v_re for g_re, g_im, v_re, v_im in parts]),
        )

    def total(a):
        return jnp.sum(a, axis=0, keepdims=True)

    first = order * BLOCKS + column
    re, im = take(gram_re, first), take(gram_im, first)
    def sweep(re, im):
        columns = [
            (take(re, order + i * ORDERS), take(im, order + i * ORDERS)) for i in range(MODES)
        ]
        for i in range(MODES):
            v_re, v_im = columns[i]
            norm = lax.rsqrt(total(v_re * v_re + v_im * v_im) + EPSILON)
            inverse = norm * norm
            for j in range(i + 1, MODES):
                u_re, u_im = columns[j]
                q_re = total(v_re * u_re + v_im * u_im) * inverse
                q_im = total(v_re * u_im - v_im * u_re) * inverse
                columns[j] = (
                    u_re - (q_re * v_re - q_im * v_im), u_im - (q_re * v_im + q_im * v_re)
                )
            columns[i] = v_re * norm, v_im * norm
        re, im = columns[0]
        for i in range(1, MODES):
            re, im = (
                jnp.where(column == i, columns[i][0], re), jnp.where(column == i, columns[i][1], im)
            )
        return re, im

    re, im = sweep(re, im)
    re, im = lax.fori_loop(1, SUBIT, lambda _, basis: sweep(*apply(*basis)), (re, im))
    image_re, image_im = apply(re, im)
    energy = total(re * image_re + im * image_im) * (1.0 / (FIELDS * CELLS * SPACE))
    energy = jnp.broadcast_to(energy, shape)

    sub = lax.broadcasted_iota(jnp.int32, (ORDERS, LANES), 0)
    lane8 = lax.broadcasted_iota(jnp.int32, (ORDERS, LANES), 1)
    table = take(energy[:ORDERS], (lane8 % MODES) * ORDERS + sub)
    energy_ref[:, 0, :] = table[:, :MODES]

    target = (lane % MODES) * ORDERS + lane // BLOCKS
    real = (lane // MODES) % 2 == 0
    out_re, out_im = take(re, target), take(im, target)
    diagonal = (
        lax.broadcasted_iota(jnp.int32, wide, 0) // BLOCKS
        == lax.broadcasted_iota(jnp.int32, wide, 1) // BLOCKS
    )
    upper = jnp.where(real, out_re, out_im)
    lower = jnp.where(real, -out_im, out_re)
    for c, part in enumerate((upper, lower)):
        block = jnp.where(diagonal, jnp.concatenate([part] * ORDERS, 0), 0.0)
        mix[:, c * LANES : (c + 1) * LANES] = block.T.astype(BF)
    factor = jnp.broadcast_to(lax.rsqrt(take(energy, target))[:1], (LANES, LANES)).T
    for n in range(WIDE // LANES):
        scale[:, n * LANES : (n + 1) * LANES] = factor

    stores = []
    for k in range(FIELDS):

        @pl.loop(0, CELLS // WIDE)
        def _(t):
            cols = pl.ds(pl.multiple_of(t * WIDE, WIDE), WIDE)
            fields = jnp.dot(mix[...], coef[k, :, cols], preferred_element_type=F32)
            fields = fields * (scale[...] * root[:, cols])
            out[:, k, :, cols] = fields.astype(BF).reshape(2 * ORDERS, MODES, WIDE)

        store = pltpu.make_async_copy(out.at[:, k], out_hbm.at[:, k], out_sem.at[k])
        store.start()
        stores.append(store)
    for store in stores:
        store.wait()


def local(records, block_start, slab_index, weight_table):
    assert records.shape == (1, TREC, FIELDS, CELLS)
    rec = jnp.transpose(records[0], (1, 0, 2))
    slab = slab_index.reshape(1, CELLS)
    hbm = pl.BlockSpec(memory_space=pltpu.HBM)
    vmem = pl.BlockSpec(memory_space=pltpu.VMEM)
    dma = pltpu.SemaphoreType.DMA
    width = 2 * ORDERS * BLOCKS
    count, chunks = len(ORDER), len(CHUNKS)
    basis, mixer = spread_time_table(), spread_order_table()
    coef, gram, weight = pl.pallas_call(
        gather_kernel,
        name="gather",
        out_shape=(
            jax.ShapeDtypeStruct((FIELDS, width, CELLS), BF),
            jax.ShapeDtypeStruct((2, BLOCKS, LANES), F32),
            jax.ShapeDtypeStruct((1, CELLS), F32),
        ),
        in_specs=[hbm] * 6,
        out_specs=(vmem, vmem, vmem),
        scratch_shapes=[
            pltpu.VMEM((FIELDS, TREC, CELLS), BF),
            pltpu.VMEM((FIELDS, NFREQ, ROWS, CELLS), BF),
            pltpu.VMEM((FIELDS, SLOTS, ROWS, CELLS), BF),
            pltpu.SMEM((BLOCKS,), jnp.int32),
            pltpu.SMEM((NSLAB,), F32),
            pltpu.VMEM((1, CELLS), jnp.int32),
            pltpu.VMEM(basis.shape, BF),
            pltpu.VMEM(mixer.shape, BF),
            pltpu.VMEM((NFREQ * ROWS, TREC), BF),
            pltpu.VMEM((BLK * NFFT, TREC), BF),
            pltpu.VMEM((width, width), F32),
            pltpu.VMEM((SPACE, 2, BLOCKS, LANES), F32),
            dma((5,)),
            dma((chunks,)),
            dma((chunks,)),
            dma((chunks, count)),
            dma((chunks, count)),
            dma((SPACE - 1,)),
            dma((SPACE - 1,)),
        ],
        compiler_params=pltpu.CompilerParams(
            collective_id=0, has_side_effects=True, vmem_limit_bytes=40 << 20
        ),
    )(*(
        pltpu.with_memory_space_constraint(a, pltpu.HBM)
        for a in (rec, block_start, weight_table, slab, jnp.asarray(basis), jnp.asarray(mixer))
    ))
    out, energy = pl.pallas_call(
        modes_kernel,
        name="modes",
        out_shape=(
            jax.ShapeDtypeStruct((2 * ORDERS, FIELDS, MODES, CELLS), BF),
            jax.ShapeDtypeStruct((ORDERS, 1, MODES), F32),
        ),
        in_specs=[vmem, vmem, vmem],
        out_specs=(hbm, vmem),
        scratch_shapes=[
            pltpu.VMEM((2 * ORDERS, FIELDS, MODES, CELLS), BF),
            pltpu.VMEM((LANES, width), BF),
            pltpu.VMEM((LANES, WIDE), F32),
            pltpu.VMEM((1, CELLS), F32),
            dma((FIELDS,)),
        ],
        compiler_params=pltpu.CompilerParams(vmem_limit_bytes=24 << 20),
    )(coef, gram, weight)
    out = out.reshape(ORDERS, 1, 2, FIELDS, MODES, CELLS)
    return jnp.transpose(out, (0, 1, 2, 4, 3, 5)), energy


def solution(mesh):
    assert dict(mesh.shape) == {"sector": SECTORS, "tm": TMS, "space": SPACE}
    placed = (P("sector", "tm", None, "space"), P(), P("space"), P())
    return jax.shard_map(
        local,
        mesh=mesh,
        in_specs=placed,
        out_specs=(
            P(None, ("sector", "tm"), None, None, None, "space"),
            P(None, ("sector", "tm"), None),
        ),
        check_vma=False,
    )
```

```python
import functools

import jax
import jax.numpy as jnp
import ml_dtypes
import numpy as np
from jax import lax
from jax.experimental import pallas as pl
from jax.experimental.pallas import tpu as pltpu
from jax.sharding import PartitionSpec as P

NFFT = 64
NFREQ = 32
MODES = 8
SUBIT = 4
EPSILON = 1e-06
MESH = pl.DeviceIdType.MESH
BF = jnp.bfloat16
F32 = jnp.float32

SECTORS = 16
ORDERS = 8
TMS = 2
SPACE = 4
BLK = 8
BLOCKS = TMS * BLK
FIELDS = 3
TREC = 296
CELLS = 2048
NSLAB = 16
SLOTS = TMS * SECTORS
ROWS = 2 * BLK
LANES = 128
WIDE = 2048
CHUNKS = ((0, 0, 2048), (1, 0, 2048), (2, 0, 2048))


def time_table():
    t = np.arange(NFFT, dtype=np.float32)
    f = np.arange(NFREQ, dtype=np.float32)
    two_pi = np.float32(2.0 * np.pi)
    window = np.float32(0.5) - np.float32(0.5) * np.cos(two_pi * t / np.float32(NFFT))
    angles = two_pi * f[:, None] * t[None, :] / np.float32(NFFT)
    both = np.stack([window * np.cos(angles), -window * np.sin(angles)])
    return (both / np.float32(np.sqrt(NFFT))).astype(ml_dtypes.bfloat16)


def order_table():
    m = np.arange(ORDERS, dtype=np.float32)[:, None]
    s = np.arange(SECTORS, dtype=np.float32)[None, :]
    angles = np.float32(2.0 * np.pi) * m * s / np.float32(SECTORS)
    cosine, sine = np.cos(angles), np.sin(angles)
    both = np.stack([np.stack([cosine, sine], -1), np.stack([-sine, cosine], -1)], 1)
    return (both / np.float32(np.sqrt(SECTORS))).astype(ml_dtypes.bfloat16)


def spread_time_table():
    basis = time_table().astype(np.float32)
    wide = np.zeros((NFREQ, BLK, 2, BLK, NFFT), np.float32)
    for b in range(BLK):
        wide[:, b, :, b, :] = basis.transpose(1, 0, 2)
    return wide.reshape(NFREQ * ROWS, BLK * NFFT).astype(ml_dtypes.bfloat16)


def spread_order_table():
    table = order_table().astype(np.float32)
    wide = np.zeros((2, ORDERS, TMS, BLK, TMS, SECTORS, BLK, 2), np.float32)
    for j in range(TMS):
        for b in range(BLK):
            wide[:, :, j, b, j, :, b, :] = table.transpose(1, 0, 2, 3)
    return wide.reshape(2 * ORDERS * BLOCKS, SLOTS * ROWS).astype(ml_dtypes.bfloat16)


def place():
    sector, tm, y = lax.axis_index("sector"), lax.axis_index("tm"), lax.axis_index("space")
    return tm * 2 + (sector // 2) % 2, y, sector // 4, sector % 2


def device_at(x, y, z, core):
    return (z * 4 + (x % 2) * 2 + core, x // 2, y)


def send_order():
    far_z, far_x = ((1, 2), (3, 2)), ((2, 1), (2, 3))
    only_x, only_z = ((2, 0),), ((0, 2),)
    common = (
        (1, 1), (3, 3), (1, 3), (3, 1), (2, 2), (1, 0), (3, 0), (0, 1), (0, 3),
    )
    zero = (*far_z, *only_x, *far_x, *only_z, *common)
    one = (*far_x, *only_z, *far_z, *only_x, *common)
    steps = [
        ((*o, c), (*p, 1 - c)) for c in range(2) for o, p in zip(zero, one, strict=True)
    ]
    return [*steps, ((0, 0, 1), (0, 0, 1))]


ORDER = send_order()


def weight_row(slab_ref, table_ref):
    slab = slab_ref[...]
    weight = jnp.zeros(slab.shape, F32)
    for n in range(NSLAB):
        weight = jnp.where(slab == n, table_ref[n], weight)
    return weight


def gather_kernel(
    rec_hbm, start_hbm, table_hbm, slab_hbm, basis_hbm, order_hbm, coef, gram_ref, weight,
    rec, send, recv, start, table, slab, basis, mixer, band, shift, acc, slots,
    in_sem, rec_sem, own_sem, send_sem, recv_sem, gsend_sem, grecv_sem,
):
    x, y, z, core = place()
    tm = x // 2
    own = tm * SECTORS + z * 4 + (x % 2) * 2 + core

    def own_offset(step):
        return tuple(p + core * (q - p) for p, q in zip(*step))

    def peer(step):
        a, b, c = own_offset(step)
        return (x + a) % 4, y, (z + b) % 4, (core + c) % 2

    def slot_of(step):
        a, b, c = own_offset(step)
        return a * 8 + b * 2 + c

    barrier = pltpu.get_barrier_semaphore()
    for offset in ORDER:
        pl.semaphore_signal(barrier, inc=1, device_id=device_at(*peer(offset)), device_id_type=MESH)
    for d in range(1, SPACE):
        pl.semaphore_signal(
            barrier, inc=1, device_id=device_at(x, (y + d) % SPACE, z, core), device_id_type=MESH
        )
    pairs = (
        (start_hbm, start), (basis_hbm, basis), (slab_hbm, slab), (table_hbm, table),
        (order_hbm, mixer),
    )
    smalls = [
        pltpu.make_async_copy(src, dst, in_sem.at[n]) for n, (src, dst) in enumerate(pairs)
    ]
    loads = [
        pltpu.make_async_copy(
            rec_hbm.at[k, :, pl.ds(first, size)], rec.at[k, :, pl.ds(first, size)], rec_sem.at[n]
        )
        for n, (k, first, size) in enumerate(CHUNKS)
    ]
    for load in (smalls[0], smalls[1], loads[0], *loads[1:], *smalls[2:]):
        load.start()
    smalls[0].wait()
    step = lax.broadcasted_iota(jnp.int32, (NFFT, TREC), 1) - lax.broadcasted_iota(
        jnp.int32, (NFFT, TREC), 0
    )
    for b in range(BLK):
        shift[b * NFFT : (b + 1) * NFFT, :] = jnp.where(
            step == start[tm * BLK + b], 1.0, 0.0
        ).astype(BF)
    smalls[1].wait()
    band[...] = jnp.dot(basis[...], shift[...], preferred_element_type=F32).astype(BF)

    copies, owns = [], []
    for n, (k, first, size) in enumerate(CHUNKS):
        loads[n].wait()
        span = pl.ds(first, size)
        out = jnp.dot(band[...], rec[k, :, span], preferred_element_type=F32)
        send[k, :, :, span] = out.astype(BF).reshape(NFREQ, ROWS, size)

        if n == 0:
            pl.semaphore_wait(barrier, len(ORDER) + SPACE - 1)
        for offset in ORDER:
            px, py, pz, pc = peer(offset)
            sector, ptm, _ = device_at(px, py, pz, pc)
            copy = pltpu.make_async_remote_copy(
                src_ref=send.at[k, sector * TMS + ptm, :, span],
                dst_ref=recv.at[k, own, :, span],
                send_sem=send_sem.at[n, slot_of(offset)],
                recv_sem=recv_sem.at[n, slot_of(offset)],
                device_id=device_at(px, py, pz, pc),
                device_id_type=MESH,
            )
            copy.start()
            copies.append(copy)
        sector, ptm, _ = device_at(x, y, z, core)
        mine = pltpu.make_async_copy(
            send.at[k, sector * TMS + ptm, :, span], recv.at[k, own, :, span], own_sem.at[n]
        )
        mine.start()
        owns.append(mine)

    for small in smalls[2:]:
        small.wait()
    weight[...] = weight_row(slab, table)
    acc[...] = jnp.zeros_like(acc)
    for n, (k, first, size) in enumerate(CHUNKS):
        for copy in copies[n * len(ORDER) : (n + 1) * len(ORDER)]:
            copy.wait_recv()
        owns[n].wait()
        span = pl.ds(first, size)
        arrived = recv[k, :, :, span].reshape(SLOTS * ROWS, size)
        c = jnp.dot(mixer[...], arrived, preferred_element_type=F32).astype(BF)
        coef[k, :, span] = c
        weighted = (c.astype(F32) * weight[:, span]).astype(BF)
        acc[...] += lax.dot_general(
            weighted, c, (((1,), (1,)), ((), ())), preferred_element_type=F32
        )

    half = ORDERS * BLOCKS
    full_re = acc[:half, :half] + acc[half:, half:]
    full_im = acc[:half, half:] - acc[half:, :half]
    group = lax.broadcasted_iota(jnp.int32, (BLOCKS, half), 1) // BLOCKS
    gram_re = jnp.zeros((BLOCKS, half), F32)
    gram_im = jnp.zeros((BLOCKS, half), F32)
    for m in range(ORDERS):
        rows = slice(m * BLOCKS, (m + 1) * BLOCKS)
        gram_re = jnp.where(group == m, full_re[rows], gram_re)
        gram_im = jnp.where(group == m, full_im[rows], gram_im)
    slots[y, 0] = gram_re
    slots[y, 1] = gram_im
    swaps = []
    for d in range(1, SPACE):
        swap = pltpu.make_async_remote_copy(
            src_ref=slots.at[y],
            dst_ref=slots.at[y],
            send_sem=gsend_sem.at[d - 1],
            recv_sem=grecv_sem.at[d - 1],
            device_id=device_at(x, (y + d) % SPACE, z, core),
            device_id_type=MESH,
        )
        swap.start()
        swaps.append(swap)
    for copy in copies:
        copy.wait_send()
    for swap in swaps:
        swap.wait_recv()
    gram_ref[...] = (slots[0] + slots[1]) + (slots[2] + slots[3])
    for swap in swaps:
        swap.wait_send()


def take(array, index):
    return jnp.take_along_axis(array, index, axis=1)


def modes_kernel(
    coef, gram_ref, weight, out_hbm, energy_ref, out, mix, scale, root, out_sem,
):
    root[...] = jnp.sqrt(weight[...])

    shape = (BLOCKS, LANES)
    lane = lax.broadcasted_iota(jnp.int32, shape, 1)
    column = (lane // ORDERS) % MODES
    order = lane % ORDERS
    gram_re, gram_im = gram_ref[0], gram_ref[1]
    wide = (BLOCKS * ORDERS, LANES)
    grid = [
        (take(gram_re, order * BLOCKS + e), take(gram_im, order * BLOCKS + e))
        for e in range(BLOCKS)
    ]

    def added(terms):
        while len(terms) > 1:
            terms = [sum(terms[n : n + 2]) for n in range(0, len(terms), 2)]
        return terms[0]

    def apply(re, im):
        parts = [
            (g_re, g_im, re[e : e + 1], im[e : e + 1]) for e, (g_re, g_im) in enumerate(grid)
        ]
        return (
            added([g_re * v_re - g_im * v_im for g_re, g_im, v_re, v_im in parts]),
            added([g_re * v_im + g_im * v_re for g_re, g_im, v_re, v_im in parts]),
        )

    def total(a):
        return jnp.sum(a, axis=0, keepdims=True)

    first = order * BLOCKS + column
    re, im = take(gram_re, first), take(gram_im, first)
    def sweep(re, im):
        columns = [
            (take(re, order + i * ORDERS), take(im, order + i * ORDERS)) for i in range(MODES)
        ]
        for i in range(MODES):
            v_re, v_im = columns[i]
            norm = lax.rsqrt(total(v_re * v_re + v_im * v_im) + EPSILON)
            inverse = norm * norm
            for j in range(i + 1, MODES):
                u_re, u_im = columns[j]
                q_re = total(v_re * u_re + v_im * u_im) * inverse
                q_im = total(v_re * u_im - v_im * u_re) * inverse
                columns[j] = (
                    u_re - (q_re * v_re - q_im * v_im), u_im - (q_re * v_im + q_im * v_re)
                )
            columns[i] = v_re * norm, v_im * norm
        re, im = columns[0]
        for i in range(1, MODES):
            re, im = (
                jnp.where(column == i, columns[i][0], re), jnp.where(column == i, columns[i][1], im)
            )
        return re, im

    re, im = sweep(re, im)
    re, im = lax.fori_loop(1, SUBIT, lambda _, basis: sweep(*apply(*basis)), (re, im))
    image_re, image_im = apply(re, im)
    energy = total(re * image_re + im * image_im) * (1.0 / (FIELDS * CELLS * SPACE))
    energy = jnp.broadcast_to(energy, shape)

    sub = lax.broadcasted_iota(jnp.int32, (ORDERS, LANES), 0)
    lane8 = lax.broadcasted_iota(jnp.int32, (ORDERS, LANES), 1)
    table = take(energy[:ORDERS], (lane8 % MODES) * ORDERS + sub)
    energy_ref[:, 0, :] = table[:, :MODES]

    target = (lane % MODES) * ORDERS + lane // BLOCKS
    real = (lane // MODES) % 2 == 0
    out_re, out_im = take(re, target), take(im, target)
    diagonal = (
        lax.broadcasted_iota(jnp.int32, wide, 0) // BLOCKS
        == lax.broadcasted_iota(jnp.int32, wide, 1) // BLOCKS
    )
    upper = jnp.where(real, out_re, out_im)
    lower = jnp.where(real, -out_im, out_re)
    for c, part in enumerate((upper, lower)):
        block = jnp.where(diagonal, jnp.concatenate([part] * ORDERS, 0), 0.0)
        mix[:, c * LANES : (c + 1) * LANES] = block.T.astype(BF)
    factor = jnp.broadcast_to(lax.rsqrt(take(energy, target))[:1], (LANES, LANES)).T
    for n in range(WIDE // LANES):
        scale[:, n * LANES : (n + 1) * LANES] = factor

    stores = []
    for k in range(FIELDS):

        @pl.loop(0, CELLS // WIDE)
        def _(t):
            cols = pl.ds(pl.multiple_of(t * WIDE, WIDE), WIDE)
            fields = jnp.dot(mix[...], coef[k, :, cols], preferred_element_type=F32)
            fields = fields * (scale[...] * root[:, cols])
            out[:, k, :, cols] = fields.astype(BF).reshape(2 * ORDERS, MODES, WIDE)

        store = pltpu.make_async_copy(out.at[:, k], out_hbm.at[:, k], out_sem.at[k])
        store.start()
        stores.append(store)
    for store in stores:
        store.wait()


def local(records, block_start, slab_index, weight_table):
    assert records.shape == (1, TREC, FIELDS, CELLS)
    rec = jnp.transpose(records[0], (1, 0, 2))
    slab = slab_index.reshape(1, CELLS)
    hbm = pl.BlockSpec(memory_space=pltpu.HBM)
    vmem = pl.BlockSpec(memory_space=pltpu.VMEM)
    dma = pltpu.SemaphoreType.DMA
    width = 2 * ORDERS * BLOCKS
    chunks = len(CHUNKS)
    basis, mixer = spread_time_table(), spread_order_table()
    coef, gram, weight = pl.pallas_call(
        gather_kernel,
        name="gather",
        out_shape=(
            jax.ShapeDtypeStruct((FIELDS, width, CELLS), BF),
            jax.ShapeDtypeStruct((2, BLOCKS, LANES), F32),
            jax.ShapeDtypeStruct((1, CELLS), F32),
        ),
        in_specs=[hbm] * 6,
        out_specs=(vmem, vmem, vmem),
        scratch_shapes=[
            pltpu.VMEM((FIELDS, TREC, CELLS), BF),
            pltpu.VMEM((FIELDS, NFREQ, ROWS, CELLS), BF),
            pltpu.VMEM((FIELDS, SLOTS, ROWS, CELLS), BF),
            pltpu.SMEM((BLOCKS,), jnp.int32),
            pltpu.SMEM((NSLAB,), F32),
            pltpu.VMEM((1, CELLS), jnp.int32),
            pltpu.VMEM(basis.shape, BF),
            pltpu.VMEM(mixer.shape, BF),
            pltpu.VMEM((NFREQ * ROWS, TREC), BF),
            pltpu.VMEM((BLK * NFFT, TREC), BF),
            pltpu.VMEM((width, width), F32),
            pltpu.VMEM((SPACE, 2, BLOCKS, LANES), F32),
            dma((5,)),
            dma((chunks,)),
            dma((chunks,)),
            dma((chunks, SLOTS)),
            dma((chunks, SLOTS)),
            dma((SPACE - 1,)),
            dma((SPACE - 1,)),
        ],
        compiler_params=pltpu.CompilerParams(
            collective_id=0, has_side_effects=True, vmem_limit_bytes=40 << 20
        ),
    )(*(
        pltpu.with_memory_space_constraint(a, pltpu.HBM)
        for a in (rec, block_start, weight_table, slab, jnp.asarray(basis), jnp.asarray(mixer))
    ))
    out, energy = pl.pallas_call(
        modes_kernel,
        name="modes",
        out_shape=(
            jax.ShapeDtypeStruct((2 * ORDERS, FIELDS, MODES, CELLS), BF),
            jax.ShapeDtypeStruct((ORDERS, 1, MODES), F32),
        ),
        in_specs=[vmem, vmem, vmem],
        out_specs=(hbm, vmem),
        scratch_shapes=[
            pltpu.VMEM((2 * ORDERS, FIELDS, MODES, CELLS), BF),
            pltpu.VMEM((LANES, width), BF),
            pltpu.VMEM((LANES, WIDE), F32),
            pltpu.VMEM((1, CELLS), F32),
            dma((FIELDS,)),
        ],
        compiler_params=pltpu.CompilerParams(vmem_limit_bytes=24 << 20),
    )(coef, gram, weight)
    out = out.reshape(ORDERS, 1, 2, FIELDS, MODES, CELLS)
    return jnp.transpose(out, (0, 1, 2, 4, 3, 5)), energy


def solution(mesh):
    assert dict(mesh.shape) == {"sector": SECTORS, "tm": TMS, "space": SPACE}
    placed = (P("sector", "tm", None, "space"), P(), P("space"), P())
    return jax.shard_map(
        local,
        mesh=mesh,
        in_specs=placed,
        out_specs=(
            P(None, ("sector", "tm"), None, None, None, "space"),
            P(None, ("sector", "tm"), None),
        ),
        check_vma=False,
    )
```

```python
import functools

import jax
import jax.numpy as jnp
import ml_dtypes
import numpy as np
from jax import lax
from jax.experimental import pallas as pl
from jax.experimental.pallas import tpu as pltpu
from jax.sharding import PartitionSpec as P

NFFT = 64
NFREQ = 32
MODES = 8
SUBIT = 4
EPSILON = 1e-06
MESH = pl.DeviceIdType.MESH
BF = jnp.bfloat16
F32 = jnp.float32

SECTORS = 16
ORDERS = 8
TMS = 2
SPACE = 4
BLK = 8
HALF = BLK // 2
BLOCKS = TMS * BLK
FIELDS = 3
TREC = 296
SECOND = HALF * NFFT // 2
SPAN = TREC - SECOND
CELLS = 2048
NSLAB = 16
SLOTS = TMS * SECTORS
ROWS = 2 * BLK
LANES = 128
WIDE = 2048
CHUNKS = ((0, 0, 2048), (1, 0, 2048), (2, 0, 2048))


def time_table():
    t = np.arange(NFFT, dtype=np.float32)
    f = np.arange(NFREQ, dtype=np.float32)
    two_pi = np.float32(2.0 * np.pi)
    window = np.float32(0.5) - np.float32(0.5) * np.cos(two_pi * t / np.float32(NFFT))
    angles = two_pi * f[:, None] * t[None, :] / np.float32(NFFT)
    both = np.stack([window * np.cos(angles), -window * np.sin(angles)])
    return (both / np.float32(np.sqrt(NFFT))).astype(ml_dtypes.bfloat16)


def order_table():
    m = np.arange(ORDERS, dtype=np.float32)[:, None]
    s = np.arange(SECTORS, dtype=np.float32)[None, :]
    angles = np.float32(2.0 * np.pi) * m * s / np.float32(SECTORS)
    cosine, sine = np.cos(angles), np.sin(angles)
    both = np.stack([np.stack([cosine, sine], -1), np.stack([-sine, cosine], -1)], 1)
    return (both / np.float32(np.sqrt(SECTORS))).astype(ml_dtypes.bfloat16)


def spread_time_table():
    basis = time_table().astype(np.float32)
    wide = np.zeros((NFREQ, HALF, 2, HALF, NFFT), np.float32)
    for b in range(HALF):
        wide[:, b, :, b, :] = basis.transpose(1, 0, 2)
    return wide.reshape(NFREQ * 2 * HALF, HALF * NFFT).astype(ml_dtypes.bfloat16)


def spread_order_table():
    table = order_table().astype(np.float32)
    wide = np.zeros((2, ORDERS, BLK, SECTORS, BLK, 2), np.float32)
    for b in range(BLK):
        wide[:, :, b, :, b, :] = table.transpose(1, 0, 2, 3)
    return wide.reshape(2 * ORDERS * BLK, SECTORS * ROWS).astype(ml_dtypes.bfloat16)


def place():
    sector, tm, y = lax.axis_index("sector"), lax.axis_index("tm"), lax.axis_index("space")
    return tm * 2 + (sector // 2) % 2, y, sector // 4, sector % 2


def device_at(x, y, z, core):
    return (z * 4 + (x % 2) * 2 + core, x // 2, y)


def send_order():
    dist = (0, 1, 2, 1)
    offsets = [
        (a, b, c) for a in range(4) for b in range(4) for c in range(2) if (a, b, c) != (0, 0, 0)
    ]
    offsets.sort(key=lambda o: -(dist[o[0]] + dist[o[1]]))
    order = []
    for a, b, c in offsets:
        for o in ((a, b, c), (-a % 4, -b % 4, c), (b, a, c), (-b % 4, -a % 4, c)):
            if o not in order:
                order.append(o)
    return order


ORDER = send_order()


def weight_row(slab_ref, table_ref):
    slab = slab_ref[...]
    weight = jnp.zeros(slab.shape, F32)
    for n in range(NSLAB):
        weight = jnp.where(slab == n, table_ref[n], weight)
    return weight


def gather_kernel(
    rec_hbm, start_hbm, table_hbm, slab_hbm, basis_hbm, order_hbm, coef, gram_ref, weight,
    rec, send, recv, start, table, slab, basis, mixer, band, shift, acc, slots,
    in_sem, rec_sem, own_sem, send_sem, recv_sem, gsend_sem, grecv_sem,
):
    x, y, z, core = place()
    tm = x // 2
    own = tm * SECTORS + z * 4 + (x % 2) * 2 + core

    def peer(offset):
        a, b, c = offset
        return (x + a + core * (b - a)) % 4, y, (z + b + core * (a - b)) % 4, (core + c) % 2

    barrier = pltpu.get_barrier_semaphore()
    for offset in ORDER:
        pl.semaphore_signal(barrier, inc=1, device_id=device_at(*peer(offset)), device_id_type=MESH)
    for d in range(1, SPACE):
        pl.semaphore_signal(
            barrier, inc=1, device_id=device_at(x, (y + d) % SPACE, z, core), device_id_type=MESH
        )
    pairs = (
        (start_hbm, start), (basis_hbm, basis), (slab_hbm, slab), (table_hbm, table),
        (order_hbm, mixer),
    )
    smalls = [
        pltpu.make_async_copy(src, dst, in_sem.at[n]) for n, (src, dst) in enumerate(pairs)
    ]
    loads = [
        pltpu.make_async_copy(
            rec_hbm.at[k, :, pl.ds(first, size)], rec.at[k, :, pl.ds(first, size)], rec_sem.at[n]
        )
        for n, (k, first, size) in enumerate(CHUNKS)
    ]
    for load in (smalls[0], smalls[1], loads[0], *loads[1:], *smalls[2:]):
        load.start()
    smalls[0].wait()
    step = lax.broadcasted_iota(jnp.int32, (NFFT, SPAN), 1) - lax.broadcasted_iota(
        jnp.int32, (NFFT, SPAN), 0
    )
    for h in range(2):
        for b in range(HALF):
            shift[h, b * NFFT : (b + 1) * NFFT, :] = jnp.where(
                step == start[tm * BLK + h * HALF + b] - h * SECOND, 1.0, 0.0
            ).astype(BF)
    smalls[1].wait()
    for h in range(2):
        band[h] = jnp.dot(basis[...], shift[h], preferred_element_type=F32).astype(BF)

    copies, owns = [], []
    for n, (k, first, size) in enumerate(CHUNKS):
        loads[n].wait()
        span = pl.ds(first, size)
        halves = [
            jnp.dot(
                band[h], rec[k, h * SECOND : h * SECOND + SPAN, span], preferred_element_type=F32
            ).reshape(NFREQ, 2 * HALF, size)
            for h in range(2)
        ]
        send[k, :, :, span] = jnp.concatenate(halves, 1).astype(BF)

        if n == 0:
            pl.semaphore_wait(barrier, len(ORDER) + SPACE - 1)
        for i, offset in enumerate(ORDER):
            px, py, pz, pc = peer(offset)
            sector, ptm, _ = device_at(px, py, pz, pc)
            copy = pltpu.make_async_remote_copy(
                src_ref=send.at[k, sector * TMS + ptm, :, span],
                dst_ref=recv.at[k, own, :, span],
                send_sem=send_sem.at[n, i],
                recv_sem=recv_sem.at[n, i],
                device_id=device_at(px, py, pz, pc),
                device_id_type=MESH,
            )
            copy.start()
            copies.append(copy)
        sector, ptm, _ = device_at(x, y, z, core)
        mine = pltpu.make_async_copy(
            send.at[k, sector * TMS + ptm, :, span], recv.at[k, own, :, span], own_sem.at[n]
        )
        mine.start()
        owns.append(mine)

    for small in smalls[2:]:
        small.wait()
    weight[...] = weight_row(slab, table)
    acc[...] = jnp.zeros_like(acc)
    for n, (k, first, size) in enumerate(CHUNKS):
        for copy in copies[n * len(ORDER) : (n + 1) * len(ORDER)]:
            copy.wait_recv()
        owns[n].wait()
        span = pl.ds(first, size)
        halves = [
            jnp.dot(
                mixer[...],
                recv[k, j * SECTORS : (j + 1) * SECTORS, :, span].reshape(SECTORS * ROWS, size),
                preferred_element_type=F32,
            ).reshape(2 * ORDERS, BLK, size)
            for j in range(TMS)
        ]
        c = jnp.concatenate(halves, 1).reshape(2 * ORDERS * BLOCKS, size).astype(BF)
        coef[k, :, span] = c
        weighted = (c.astype(F32) * weight[:, span]).astype(BF)
        acc[...] += lax.dot_general(
            weighted, c, (((1,), (1,)), ((), ())), preferred_element_type=F32
        )

    half = ORDERS * BLOCKS
    full_re = acc[:half, :half] + acc[half:, half:]
    full_im = acc[:half, half:] - acc[half:, :half]
    group = lax.broadcasted_iota(jnp.int32, (BLOCKS, half), 1) // BLOCKS
    gram_re = jnp.zeros((BLOCKS, half), F32)
    gram_im = jnp.zeros((BLOCKS, half), F32)
    for m in range(ORDERS):
        rows = slice(m * BLOCKS, (m + 1) * BLOCKS)
        gram_re = jnp.where(group == m, full_re[rows], gram_re)
        gram_im = jnp.where(group == m, full_im[rows], gram_im)
    slots[y, 0] = gram_re
    slots[y, 1] = gram_im
    swaps = []
    for d in range(1, SPACE):
        swap = pltpu.make_async_remote_copy(
            src_ref=slots.at[y],
            dst_ref=slots.at[y],
            send_sem=gsend_sem.at[d - 1],
            recv_sem=grecv_sem.at[d - 1],
            device_id=device_at(x, (y + d) % SPACE, z, core),
            device_id_type=MESH,
        )
        swap.start()
        swaps.append(swap)
    for copy in copies:
        copy.wait_send()
    for swap in swaps:
        swap.wait_recv()
    gram_ref[...] = (slots[0] + slots[1]) + (slots[2] + slots[3])
    for swap in swaps:
        swap.wait_send()


def take(array, index):
    return jnp.take_along_axis(array, index, axis=1)


def modes_kernel(
    coef, gram_ref, weight, out_hbm, energy_ref, out, mix, scale, root, out_sem,
):
    root[...] = jnp.sqrt(weight[...])

    shape = (BLOCKS, LANES)
    lane = lax.broadcasted_iota(jnp.int32, shape, 1)
    column = (lane // ORDERS) % MODES
    order = lane % ORDERS
    gram_re, gram_im = gram_ref[0], gram_ref[1]
    wide = (BLOCKS * ORDERS, LANES)
    grid = [
        (take(gram_re, order * BLOCKS + e), take(gram_im, order * BLOCKS + e))
        for e in range(BLOCKS)
    ]

    def added(terms):
        while len(terms) > 1:
            terms = [sum(terms[n : n + 2]) for n in range(0, len(terms), 2)]
        return terms[0]

    def apply(re, im):
        parts = [
            (g_re, g_im, re[e : e + 1], im[e : e + 1]) for e, (g_re, g_im) in enumerate(grid)
        ]
        return (
            added([g_re * v_re - g_im * v_im for g_re, g_im, v_re, v_im in parts]),
            added([g_re * v_im + g_im * v_re for g_re, g_im, v_re, v_im in parts]),
        )

    def total(a):
        return jnp.sum(a, axis=0, keepdims=True)

    first = order * BLOCKS + column
    re, im = take(gram_re, first), take(gram_im, first)
    def sweep(re, im):
        columns = [
            (take(re, order + i * ORDERS), take(im, order + i * ORDERS)) for i in range(MODES)
        ]
        for i in range(MODES):
            v_re, v_im = columns[i]
            norm = lax.rsqrt(total(v_re * v_re + v_im * v_im) + EPSILON)
            inverse = norm * norm
            for j in range(i + 1, MODES):
                u_re, u_im = columns[j]
                q_re = total(v_re * u_re + v_im * u_im) * inverse
                q_im = total(v_re * u_im - v_im * u_re) * inverse
                columns[j] = (
                    u_re - (q_re * v_re - q_im * v_im), u_im - (q_re * v_im + q_im * v_re)
                )
            columns[i] = v_re * norm, v_im * norm
        re, im = columns[0]
        for i in range(1, MODES):
            re, im = (
                jnp.where(column == i, columns[i][0], re), jnp.where(column == i, columns[i][1], im)
            )
        return re, im

    re, im = sweep(re, im)
    re, im = lax.fori_loop(1, SUBIT, lambda _, basis: sweep(*apply(*basis)), (re, im))
    image_re, image_im = apply(re, im)
    energy = total(re * image_re + im * image_im) * (1.0 / (FIELDS * CELLS * SPACE))
    energy = jnp.broadcast_to(energy, shape)

    sub = lax.broadcasted_iota(jnp.int32, (ORDERS, LANES), 0)
    lane8 = lax.broadcasted_iota(jnp.int32, (ORDERS, LANES), 1)
    table = take(energy[:ORDERS], (lane8 % MODES) * ORDERS + sub)
    energy_ref[:, 0, :] = table[:, :MODES]

    target = (lane % MODES) * ORDERS + lane // BLOCKS
    real = (lane // MODES) % 2 == 0
    out_re, out_im = take(re, target), take(im, target)
    diagonal = (
        lax.broadcasted_iota(jnp.int32, wide, 0) // BLOCKS
        == lax.broadcasted_iota(jnp.int32, wide, 1) // BLOCKS
    )
    upper = jnp.where(real, out_re, out_im)
    lower = jnp.where(real, -out_im, out_re)
    for c, part in enumerate((upper, lower)):
        block = jnp.where(diagonal, jnp.concatenate([part] * ORDERS, 0), 0.0)
        mix[:, c * LANES : (c + 1) * LANES] = block.T.astype(BF)
    factor = jnp.broadcast_to(lax.rsqrt(take(energy, target))[:1], (LANES, LANES)).T
    for n in range(WIDE // LANES):
        scale[:, n * LANES : (n + 1) * LANES] = factor

    stores = []
    for k in range(FIELDS):

        @pl.loop(0, CELLS // WIDE)
        def _(t):
            cols = pl.ds(pl.multiple_of(t * WIDE, WIDE), WIDE)
            fields = jnp.dot(mix[...], coef[k, :, cols], preferred_element_type=F32)
            fields = fields * (scale[...] * root[:, cols])
            out[:, k, :, cols] = fields.astype(BF).reshape(2 * ORDERS, MODES, WIDE)

        store = pltpu.make_async_copy(out.at[:, k], out_hbm.at[:, k], out_sem.at[k])
        store.start()
        stores.append(store)
    for store in stores:
        store.wait()


def local(records, block_start, slab_index, weight_table):
    assert records.shape == (1, TREC, FIELDS, CELLS)
    rec = jnp.transpose(records[0], (1, 0, 2))
    slab = slab_index.reshape(1, CELLS)
    hbm = pl.BlockSpec(memory_space=pltpu.HBM)
    vmem = pl.BlockSpec(memory_space=pltpu.VMEM)
    dma = pltpu.SemaphoreType.DMA
    width = 2 * ORDERS * BLOCKS
    count, chunks = len(ORDER), len(CHUNKS)
    basis, mixer = spread_time_table(), spread_order_table()
    coef, gram, weight = pl.pallas_call(
        gather_kernel,
        name="gather",
        out_shape=(
            jax.ShapeDtypeStruct((FIELDS, width, CELLS), BF),
            jax.ShapeDtypeStruct((2, BLOCKS, LANES), F32),
            jax.ShapeDtypeStruct((1, CELLS), F32),
        ),
        in_specs=[hbm] * 6,
        out_specs=(vmem, vmem, vmem),
        scratch_shapes=[
            pltpu.VMEM((FIELDS, TREC, CELLS), BF),
            pltpu.VMEM((FIELDS, NFREQ, ROWS, CELLS), BF),
            pltpu.VMEM((FIELDS, SLOTS, ROWS, CELLS), BF),
            pltpu.SMEM((BLOCKS,), jnp.int32),
            pltpu.SMEM((NSLAB,), F32),
            pltpu.VMEM((1, CELLS), jnp.int32),
            pltpu.VMEM(basis.shape, BF),
            pltpu.VMEM(mixer.shape, BF),
            pltpu.VMEM((2, NFREQ * 2 * HALF, SPAN), BF),
            pltpu.VMEM((2, HALF * NFFT, SPAN), BF),
            pltpu.VMEM((width, width), F32),
            pltpu.VMEM((SPACE, 2, BLOCKS, LANES), F32),
            dma((5,)),
            dma((chunks,)),
            dma((chunks,)),
            dma((chunks, count)),
            dma((chunks, count)),
            dma((SPACE - 1,)),
            dma((SPACE - 1,)),
        ],
        compiler_params=pltpu.CompilerParams(
            collective_id=0, has_side_effects=True, vmem_limit_bytes=40 << 20
        ),
    )(*(
        pltpu.with_memory_space_constraint(a, pltpu.HBM)
        for a in (rec, block_start, weight_table, slab, jnp.asarray(basis), jnp.asarray(mixer))
    ))
    out, energy = pl.pallas_call(
        modes_kernel,
        name="modes",
        out_shape=(
            jax.ShapeDtypeStruct((2 * ORDERS, FIELDS, MODES, CELLS), BF),
            jax.ShapeDtypeStruct((ORDERS, 1, MODES), F32),
        ),
        in_specs=[vmem, vmem, vmem],
        out_specs=(hbm, vmem),
        scratch_shapes=[
            pltpu.VMEM((2 * ORDERS, FIELDS, MODES, CELLS), BF),
            pltpu.VMEM((LANES, width), BF),
            pltpu.VMEM((LANES, WIDE), F32),
            pltpu.VMEM((1, CELLS), F32),
            dma((FIELDS,)),
        ],
        compiler_params=pltpu.CompilerParams(vmem_limit_bytes=24 << 20),
    )(coef, gram, weight)
    out = out.reshape(ORDERS, 1, 2, FIELDS, MODES, CELLS)
    return jnp.transpose(out, (0, 1, 2, 4, 3, 5)), energy


def solution(mesh):
    assert dict(mesh.shape) == {"sector": SECTORS, "tm": TMS, "space": SPACE}
    placed = (P("sector", "tm", None, "space"), P(), P("space"), P())
    return jax.shard_map(
        local,
        mesh=mesh,
        in_specs=placed,
        out_specs=(
            P(None, ("sector", "tm"), None, None, None, "space"),
            P(None, ("sector", "tm"), None),
        ),
        check_vma=False,
    )
```
